32 devices in a mesh: rep: 4 (over y, x), shard: 8 (over z, core).
Axes of the slice: x: 2, y: 2, z: 4, core: 2. Of those that a mesh axis runs over, the one named last changes fastest.
Arguments:
- hidden_in: bfloat16 [8, 512, 768], P('shard', 'rep')
- attn_in: bfloat16 [1, 768, 2304], P(None, 'shard')
- attn_out: bfloat16 [1, 768, 768], P(None, 'shard'), may hold values from -4 to 4
- fc_in: bfloat16 [1, 768, 3072], P(None, 'shard'), may hold values from -0.21875 to 0.21875
- fc_out: bfloat16 [1, 3072, 768], P(None, 'shard'), may hold values from -0.109375 to 0.109375
- norm_gains: bfloat16 [1, 2, 768], P(None, None, 'shard'), may hold values from 0.099609375 to 1.8984375
- biases: bfloat16 [1, 6, 768], P(None, None, 'shard'), may hold values from -3 to 3
- fc_in_bias: bfloat16 [1, 3072], P(None, 'shard'), may hold values from -3 to 3
- out_grad: float32 [8, 512, 768], P('shard', 'rep'), may hold values from -6 to 6
Outputs:
- hidden_out: float32 [8, 512, 768], P('shard', 'rep')
- hidden_in_grad: float32 [8, 512, 768], P('shard', 'rep')
- attn_in_grad: float32 [1, 768, 2304], P(None, 'shard')
- attn_out_grad: float32 [1, 768, 768], P(None, 'shard')
- fc_in_grad: float32 [1, 768, 3072], P(None, 'shard')
- fc_out_grad: float32 [1, 3072, 768], P(None, 'shard')
- norm_gains_grad: float32 [1, 2, 768], P(None, None, 'shard')
- biases_grad: float32 [1, 6, 768], P(None, None, 'shard')
- fc_in_bias_grad: float32 [1, 3072], P(None, 'shard')
The draws below stay inside these ranges and needn't reach their ends.
All inputs are finite; a program needn't handle non-finite values.
Results may differ from the reference program's by a relative error of at most 0.019.
The reference program's roundings to bfloat16 on the way count: a program that leaves them out, or rounds other values in their place, can miss the bound.
Values may be sent and summed in bfloat16 or wider, within the bound.
A program may use at most 128 MiB of HBM per device.

```python
import math
import jax
import jax.numpy as jnp
from jax import lax

D = 768
H = 12
FF = 3072
LAYERS = 1
CLIP = 512
CLIPS = 8


def draw_hidden_in(key, part):
    first = jax.random.fold_in(key, 0)
    return jnp.clip(jax.random.normal(first, (CLIPS, CLIP, D), jnp.float32), -5.0, 5.0).astype(jnp.bfloat16)


def draw_attn_in(key, part):
    first, second, third = jax.random.split(key, 3)
    scale = D ** (-0.5)
    keys_part = jnp.clip(jax.random.normal(second, (LAYERS, D, D), jnp.float32), -5.0, 5.0) * scale
    values_part = jnp.clip(jax.random.normal(third, (LAYERS, D, D), jnp.float32), -5.0, 5.0) * scale
    noise = jnp.clip(jax.random.normal(first, (LAYERS, D, D), jnp.float32), -5.0, 5.0) * scale
    queries_part = noise
    return jnp.concatenate([queries_part, keys_part, values_part], axis=2).astype(jnp.bfloat16)


def steps_of(stream_key, shape, cuts, low, largest):
    def one(axis_at, parts):
        heights = jax.random.uniform(jax.random.fold_in(jax.random.fold_in(stream_key, 6), axis_at), (parts,), jnp.float32, low / len(cuts), largest / len(cuts))
        return jnp.repeat(jnp.exp(heights), shape[axis_at] // parts).reshape((-1,) + (1,) * (len(shape) - axis_at - 1))

    level = one(*cuts[0])
    for cut in cuts[1:]:
        level = level * one(*cut)
    return level


def gaussian(stream_key, dims, scale, reach, shards=(), held_as=jnp.bfloat16):
    values = jax.random.normal(stream_key, dims, jnp.float32) * scale
    if len(shards) > 0:
        values = steps_of(stream_key, dims, shards, -0.22, 0.18) * values
    return jnp.clip(values, min=-reach, max=reach).astype(held_as)


def setup_inputs(seed: int = 0) -> dict:
    key_list = jax.random.split(jax.random.key(seed), 10)
    return {
        "hidden_in": draw_hidden_in(jax.random.fold_in(key_list[9], 71), 0),
        "attn_in": draw_attn_in(jax.random.fold_in(key_list[9], 71), 0),
        "attn_out": gaussian(key_list[2], (LAYERS, D, D), 2 ** -0.5, 4.0, ((1, 8),)),
        "fc_in": gaussian(key_list[3], (LAYERS, D, FF), D ** -0.5, 0.21875, ((1, 8),)),
        "fc_out": gaussian(key_list[4], (LAYERS, FF, D), FF ** -0.5, 0.109375, ((1, 8),)),
        "norm_gains": jnp.clip(1.0 + 0.18 * jax.random.normal(key_list[5], (LAYERS, 2, D), jnp.float32), 0.099609375, 1.8984375).astype(jnp.bfloat16),
        "biases": gaussian(key_list[6], (LAYERS, 6, D), 0.5, 3.0, ((2, 8),)),
        "fc_in_bias": gaussian(key_list[7], (LAYERS, FF), 0.5, 3.0, ((1, 8),)),
        "out_grad": gaussian(key_list[8], (CLIPS, CLIP, D), 1.0, 6.0, ((0, 8), (1, 4)), jnp.float32),
    }


EPS = 1e-05

def norm_forward(values, gain, shift):
    center = values - lax.optimization_barrier(jnp.mean(values, axis=-1, keepdims=True))
    inv_root = lax.rsqrt(lax.optimization_barrier(jnp.mean(center * center, axis=-1, keepdims=True)) + EPS)
    normed = center * inv_root
    return (normed * gain + shift, normed, inv_root)

def norm_backward(upstream, gain, normed, inv_root):
    scaled = upstream * gain
    inner = scaled - lax.optimization_barrier(jnp.mean(scaled, axis=-1, keepdims=True)) - normed * lax.optimization_barrier(jnp.mean(scaled * normed, axis=-1, keepdims=True))
    return (inv_root * inner, lax.optimization_barrier(jnp.sum(upstream * normed, axis=0)), lax.optimization_barrier(jnp.sum(upstream, axis=0)))

def gelu_slope(pre):
    cdf = 0.5 * (1.0 + lax.erf(pre * (1.0 / math.sqrt(2.0))))
    dens = jnp.exp(-0.5 * pre * pre) * (1.0 / math.sqrt(2.0 * math.pi))
    return cdf + pre * dens

def split_heads(values):
    return values.reshape(values.shape[0], H, values.shape[1] // H).astype(jnp.float32)

def score_block(queries, keys):
    scale = (queries.shape[1] // H) ** (-0.5)
    return jnp.einsum('qhd,khd->hqk', split_heads(queries), split_heads(keys)) * scale

def attend(queries, keys, values_in):
    scores = score_block(queries, keys)
    top = lax.optimization_barrier(jnp.max(scores, axis=-1, keepdims=True))
    lse = top[..., 0] + jnp.log(lax.optimization_barrier(jnp.sum(jnp.exp(scores - top), axis=-1)))
    probs = jnp.exp(scores - lse[..., None]).astype(jnp.bfloat16)
    mixed = jnp.einsum('hqk,khd->qhd', probs.astype(jnp.float32), split_heads(values_in))
    return (mixed.reshape(queries.shape[0], -1).astype(jnp.bfloat16), lse)

def attend_back(queries, keys, values_in, lse, upstream):
    scale = (queries.shape[1] // H) ** (-0.5)
    probs = jnp.exp(score_block(queries, keys) - lse[..., None])
    weights = probs.astype(jnp.bfloat16).astype(jnp.float32)
    dprobs = jnp.einsum('qhd,khd->hqk', split_heads(upstream), split_heads(values_in))
    delta = lax.optimization_barrier(jnp.sum(probs * dprobs, axis=-1, keepdims=True))
    dscores = (probs * (dprobs - delta) * scale).astype(jnp.bfloat16).astype(jnp.float32)
    dquery = jnp.einsum('hqk,khd->qhd', dscores, split_heads(keys)).reshape(queries.shape[0], -1)
    dkey = jnp.einsum('hqk,qhd->khd', dscores, split_heads(queries)).reshape(keys.shape[0], -1)
    dvalue = jnp.einsum('hqk,qhd->khd', weights, split_heads(upstream)).reshape(keys.shape[0], -1)
    return (dquery, dkey, dvalue)

def clip_pass(clip_in, clip_grad, attn_in, attn_out, fc_in, fc_out, norm_gains, biases, fc_in_bias):
    state = clip_in.astype(jnp.float32)
    width = state.shape[1]
    saved = []
    for layer in range(LAYERS):
        gains = norm_gains[layer].astype(jnp.float32)
        shifts = biases[layer].astype(jnp.float32)
        up_bias = fc_in_bias[layer].astype(jnp.float32)
        normed_in, normed1, inv1 = norm_forward(state, gains[0], shifts[0])
        a_low = normed_in.astype(jnp.bfloat16)
        qkv = jnp.dot(a_low, attn_in[layer], preferred_element_type=jnp.float32)
        queries = (qkv[:, :width] + shifts[1]).astype(jnp.bfloat16)
        keys = qkv[:, width:2 * width].astype(jnp.bfloat16)
        values_in = (qkv[:, 2 * width:] + shifts[2]).astype(jnp.bfloat16)
        attended, lse = attend(queries, keys, values_in)
        mixed = state + jnp.dot(attended, attn_out[layer], preferred_element_type=jnp.float32) + shifts[3]
        normed_mid, normed2, inv2 = norm_forward(mixed, gains[1], shifts[4])
        c_low = normed_mid.astype(jnp.bfloat16)
        pre = jnp.dot(c_low, fc_in[layer], preferred_element_type=jnp.float32) + up_bias
        act_low = jax.nn.gelu(pre, approximate=False).astype(jnp.bfloat16)
        result = mixed + jnp.dot(act_low, fc_out[layer], preferred_element_type=jnp.float32) + shifts[5]
        saved.append((normed1, inv1, a_low, queries, keys, values_in, lse, attended, normed2, inv2, c_low, pre, act_low))
        state = result
    upstream = clip_grad.astype(jnp.float32)
    layer_grads = [None] * LAYERS
    for layer in reversed(range(LAYERS)):
        normed1, inv1, a_low, queries, keys, values_in, lse, attended, normed2, inv2, c_low, pre, act_low = saved[layer]
        gains = norm_gains[layer].astype(jnp.float32)
        dy_low = upstream.astype(jnp.bfloat16)
        d_down = jnp.dot(act_low.T, dy_low, preferred_element_type=jnp.float32)
        de5 = lax.optimization_barrier(jnp.sum(upstream, axis=0))
        dact = jnp.dot(dy_low, fc_out[layer].T, preferred_element_type=jnp.float32)
        dpre = dact * gelu_slope(pre)
        dpre_low = dpre.astype(jnp.bfloat16)
        d_up = jnp.dot(c_low.T, dpre_low, preferred_element_type=jnp.float32)
        d_up_bias = lax.optimization_barrier(jnp.sum(dpre, axis=0))
        dmid = jnp.dot(dpre_low, fc_in[layer].T, preferred_element_type=jnp.float32)
        dmixed_part, dg2, de4 = norm_backward(dmid, gains[1], normed2, inv2)
        dmixed = upstream + dmixed_part
        dmixed_low = dmixed.astype(jnp.bfloat16)
        d_out = jnp.dot(attended.T, dmixed_low, preferred_element_type=jnp.float32)
        de3 = lax.optimization_barrier(jnp.sum(dmixed, axis=0))
        dattended = jnp.dot(dmixed_low, attn_out[layer].T, preferred_element_type=jnp.float32).astype(jnp.bfloat16)
        dquery, dkey, dvalue = attend_back(queries, keys, values_in, lse, dattended)
        g_qkv = jnp.concatenate([dquery, dkey, dvalue], axis=1).astype(jnp.bfloat16)
        d_qkv = jnp.dot(a_low.T, g_qkv, preferred_element_type=jnp.float32)
        de1 = lax.optimization_barrier(jnp.sum(dquery, axis=0))
        de2 = lax.optimization_barrier(jnp.sum(dvalue, axis=0))
        dnormed = jnp.dot(g_qkv, attn_in[layer].T, preferred_element_type=jnp.float32)
        dstate_part, dg1, de0 = norm_backward(dnormed, gains[0], normed1, inv1)
        upstream = dmixed + dstate_part
        layer_grads[layer] = (d_qkv, d_out, d_up, d_down, jnp.stack([dg1, dg2]), jnp.stack([de0, de1, de2, de3, de4, de5]), d_up_bias)
    stacked = tuple((jnp.stack([grads[index] for grads in layer_grads]) for index in range(7)))
    return (state, upstream, stacked)

def reference(hidden_in, attn_in, attn_out, fc_in, fc_out, norm_gains, biases, fc_in_bias, out_grad):

    def step(totals, pair):
        result, dinput, grads = clip_pass(pair[0], pair[1], attn_in, attn_out, fc_in, fc_out, norm_gains, biases, fc_in_bias)
        return (tuple((total + grad for total, grad in zip(totals, grads))), (result, dinput))
    shapes = (attn_in.shape, attn_out.shape, fc_in.shape, fc_out.shape, norm_gains.shape, biases.shape, fc_in_bias.shape)
    zeros = tuple((jnp.zeros(shape, jnp.float32) for shape in shapes))
    totals, (results, dinputs) = lax.scan(step, zeros, (hidden_in, out_grad))
    return (results, dinputs, totals[0], totals[1], totals[2], totals[3], totals[4], totals[5], totals[6])
```

```python
import functools
import math

import jax
import jax.numpy as jnp
from jax import lax
from jax.experimental import pallas as pl
from jax.experimental.pallas import tpu as pltpu
from jax.sharding import PartitionSpec as P

H = 12

BF16 = jnp.bfloat16
F32 = jnp.float32


EPS = 1e-05


def norm_forward(values, gain, shift):
    center = values - jnp.mean(values, axis=-1, keepdims=True)
    inv_root = lax.rsqrt(jnp.mean(center * center, axis=-1, keepdims=True) + EPS)
    normed = center * inv_root
    return (normed * gain + shift, normed, inv_root)


def norm_backward(upstream, gain, normed, inv_root):
    scaled = upstream * gain
    inner = (
        scaled
        - jnp.mean(scaled, axis=-1, keepdims=True)
        - normed * jnp.mean(scaled * normed, axis=-1, keepdims=True)
    )
    return (inv_root * inner, jnp.sum(upstream * normed, axis=0), jnp.sum(upstream, axis=0))


def gelu_slope(pre):
    cdf = 0.5 * (1.0 + lax.erf(pre * (1.0 / math.sqrt(2.0))))
    dens = jnp.exp(-0.5 * pre * pre) * (1.0 / math.sqrt(2.0 * math.pi))
    return cdf + pre * dens


def contract_rows(left, right):
    return lax.dot_general(
        left, right, (((0,), (0,)), ((), ())), preferred_element_type=jnp.float32
    )


def contract_cols(left, right):
    return lax.dot_general(
        left, right, (((1,), (1,)), ((), ())), preferred_element_type=jnp.float32
    )


def split_heads(values):
    return values.reshape(values.shape[0], H, values.shape[1] // H)


def score_block(queries, keys):
    scale = (queries.shape[1] // H) ** (-0.5)
    return (
        jnp.einsum(
            "qhd,khd->hqk",
            split_heads(queries),
            split_heads(keys),
            preferred_element_type=jnp.float32,
        )
        * scale
    )


def attend(queries, keys, values_in):
    scores = score_block(queries, keys)
    top = jnp.max(scores, axis=-1, keepdims=True)
    lse = top[..., 0] + jnp.log(jnp.sum(jnp.exp(scores - top), axis=-1))
    probs = jnp.exp(scores - lse[..., None]).astype(jnp.bfloat16)
    mixed = jnp.einsum(
        "hqk,khd->qhd", probs, split_heads(values_in), preferred_element_type=jnp.float32
    )
    return (mixed.reshape(queries.shape[0], -1).astype(jnp.bfloat16), lse)


def attend_back(queries, keys, values_in, lse, upstream):
    scale = (queries.shape[1] // H) ** (-0.5)
    probs = jnp.exp(score_block(queries, keys) - lse[..., None])
    weights = probs.astype(jnp.bfloat16)
    dprobs = jnp.einsum(
        "qhd,khd->hqk",
        split_heads(upstream),
        split_heads(values_in),
        preferred_element_type=jnp.float32,
    )
    delta = jnp.sum(probs * dprobs, axis=-1, keepdims=True)
    dscores = (probs * (dprobs - delta) * scale).astype(jnp.bfloat16)
    dquery = jnp.einsum(
        "hqk,khd->qhd", dscores, split_heads(keys), preferred_element_type=jnp.float32
    ).reshape(queries.shape[0], -1)
    dkey = jnp.einsum(
        "hqk,qhd->khd", dscores, split_heads(queries), preferred_element_type=jnp.float32
    ).reshape(keys.shape[0], -1)
    dvalue = jnp.einsum(
        "hqk,qhd->khd", weights, split_heads(upstream), preferred_element_type=jnp.float32
    ).reshape(keys.shape[0], -1)
    return (dquery, dkey, dvalue)


def body(hidden_in, attn_in, attn_out, fc_in, fc_out, norm_gains, biases, fc_in_bias, out_grad):
    layers = attn_in.shape[0]
    state = hidden_in[0].astype(jnp.float32)
    layer = 0
    pieces = (
        lax.all_gather(attn_in[layer], "shard", axis=0, tiled=True),
        lax.all_gather(attn_out[layer], "shard", axis=0, tiled=True),
        lax.all_gather(fc_in[layer], "shard", axis=0, tiled=True),
        lax.all_gather(fc_out[layer], "shard", axis=0, tiled=True),
        lax.all_gather(norm_gains[layer], "shard", axis=1, tiled=True),
        lax.all_gather(biases[layer], "shard", axis=1, tiled=True),
        lax.all_gather(fc_in_bias[layer], "shard", axis=0, tiled=True),
    )
    w_qkv = pieces[0]
    w_out = pieces[1]
    w_up = pieces[2]
    w_down = pieces[3]
    gains = pieces[4].astype(jnp.float32)
    shifts = pieces[5].astype(jnp.float32)
    up_bias = pieces[6].astype(jnp.float32)
    width = w_out.shape[0]
    normed_in, normed1, inv1 = norm_forward(state, gains[0], shifts[0])
    a_low = normed_in.astype(jnp.bfloat16)
    qkv = jnp.dot(a_low, w_qkv, preferred_element_type=jnp.float32)
    queries = (qkv[:, :width] + shifts[1]).astype(jnp.bfloat16)
    keys_local = qkv[:, width : 2 * width].astype(jnp.bfloat16)
    values_local = (qkv[:, 2 * width :] + shifts[2]).astype(jnp.bfloat16)
    keys_all = lax.all_gather(keys_local, "rep", axis=0, tiled=True)
    values_all = lax.all_gather(values_local, "rep", axis=0, tiled=True)
    attended, lse = attend(queries, keys_all, values_all)
    mixed = state + jnp.dot(attended, w_out, preferred_element_type=jnp.float32) + shifts[3]
    normed_mid, normed2, inv2 = norm_forward(mixed, gains[1], shifts[4])
    c_low = normed_mid.astype(jnp.bfloat16)
    pre = jnp.dot(c_low, w_up, preferred_element_type=jnp.float32) + up_bias
    act_low = jax.nn.gelu(pre, approximate=False).astype(jnp.bfloat16)
    result = mixed + jnp.dot(act_low, w_down, preferred_element_type=jnp.float32) + shifts[5]
    saved = [
        (
            normed1,
            inv1,
            a_low,
            queries,
            keys_all,
            values_all,
            lse,
            attended,
            normed2,
            inv2,
            c_low,
            pre,
            act_low,
            (w_qkv, w_out, w_up, w_down, gains),
        )
    ]
    upstream = out_grad[0]
    layer_grads = [None] * layers
    for layer in reversed(range(layers)):
        (
            normed1,
            inv1,
            a_low,
            queries,
            keys_all,
            values_all,
            lse,
            attended,
            normed2,
            inv2,
            c_low,
            pre,
            act_low,
            held,
        ) = saved[layer]
        w_qkv, w_out, w_up, w_down, gains = held
        dy_low = upstream.astype(jnp.bfloat16)
        d_down = contract_rows(act_low, dy_low)
        de5 = jnp.sum(upstream, axis=0)
        dact = contract_cols(dy_low, w_down)
        dpre = dact * gelu_slope(pre)
        dpre_low = dpre.astype(jnp.bfloat16)
        d_up = contract_rows(c_low, dpre_low)
        d_up_bias = jnp.sum(dpre, axis=0)
        dmid = contract_cols(dpre_low, w_up)
        dmixed_part, dg2, de4 = norm_backward(dmid, gains[1], normed2, inv2)
        dmixed = upstream + dmixed_part
        dmixed_low = dmixed.astype(jnp.bfloat16)
        d_out = contract_rows(attended, dmixed_low)
        de3 = jnp.sum(dmixed, axis=0)
        dattended = contract_cols(dmixed_low, w_out).astype(jnp.bfloat16)
        dquery, dkey_part, dvalue_part = attend_back(queries, keys_all, values_all, lse, dattended)
        dkey, dvalue = (
            lax.psum_scatter(
                dkey_part.astype(jnp.bfloat16), "rep", scatter_dimension=0, tiled=True
            ).astype(jnp.float32),
            lax.psum_scatter(
                dvalue_part.astype(jnp.bfloat16), "rep", scatter_dimension=0, tiled=True
            ).astype(jnp.float32),
        )
        g_qkv = jnp.concatenate([dquery, dkey, dvalue], axis=1).astype(jnp.bfloat16)
        d_qkv = contract_rows(a_low, g_qkv)
        de1 = jnp.sum(dquery, axis=0)
        de2 = jnp.sum(dvalue, axis=0)
        dnormed = contract_cols(g_qkv, w_qkv)
        dstate_part, dg1, de0 = norm_backward(dnormed, gains[0], normed1, inv1)
        upstream = dmixed + dstate_part
        owned = (
            lax.psum_scatter(
                d_qkv.astype(jnp.bfloat16), "shard", scatter_dimension=0, tiled=True
            ).astype(jnp.float32),
            lax.psum_scatter(
                d_out.astype(jnp.bfloat16), "shard", scatter_dimension=0, tiled=True
            ).astype(jnp.float32),
            lax.psum_scatter(
                d_up.astype(jnp.bfloat16), "shard", scatter_dimension=0, tiled=True
            ).astype(jnp.float32),
            lax.psum_scatter(
                d_down.astype(jnp.bfloat16), "shard", scatter_dimension=0, tiled=True
            ).astype(jnp.float32),
            lax.psum_scatter(
                jnp.stack([dg1, dg2]).astype(jnp.bfloat16), "shard", scatter_dimension=1, tiled=True
            ).astype(jnp.float32),
            lax.psum_scatter(
                jnp.stack([de0, de1, de2, de3, de4, de5]).astype(jnp.bfloat16),
                "shard",
                scatter_dimension=1,
                tiled=True,
            ).astype(jnp.float32),
            lax.psum_scatter(
                d_up_bias.astype(jnp.bfloat16), "shard", scatter_dimension=0, tiled=True
            ).astype(jnp.float32),
        )
        owned = (
            lax.psum(owned[0].astype(jnp.bfloat16), "rep").astype(jnp.float32),
            lax.psum(owned[1].astype(jnp.bfloat16), "rep").astype(jnp.float32),
            lax.psum(owned[2].astype(jnp.bfloat16), "rep").astype(jnp.float32),
            lax.psum(owned[3].astype(jnp.bfloat16), "rep").astype(jnp.float32),
            lax.psum(owned[4].astype(jnp.bfloat16), "rep").astype(jnp.float32),
            lax.psum(owned[5].astype(jnp.bfloat16), "rep").astype(jnp.float32),
            lax.psum(owned[6].astype(jnp.bfloat16), "rep").astype(jnp.float32),
        )
        layer_grads[layer] = owned
    stacked = tuple((jnp.stack([grads[index] for grads in layer_grads]) for index in range(7)))
    return (
        result[None],
        upstream[None],
        stacked[0],
        stacked[1],
        stacked[2],
        stacked[3],
        stacked[4],
        stacked[5],
        stacked[6],
    )


def exchange_body(plan, sizes, *refs):
    count = len(plan)
    ins, outs = refs[:count], refs[count : 2 * count]
    send_sem, recv_sem = refs[2 * count :]
    me = {axis: lax.axis_index(axis) for axis in sizes}
    barrier = pltpu.get_barrier_semaphore()
    greeted = 0
    for axis in sorted({axis for axis, _ in plan}):
        for step in range(1, sizes[axis]):
            peer = lax.rem(me[axis] + step, sizes[axis])
            pl.semaphore_signal(
                barrier, inc=1, device_id={axis: peer}, device_id_type=pl.DeviceIdType.MESH
            )
            greeted += 1
    pl.semaphore_wait(barrier, greeted)

    def copy(item, slot, source, target, axis, peer):
        return pltpu.make_async_remote_copy(
            src_ref=source,
            dst_ref=target,
            send_sem=send_sem.at[item, slot],
            recv_sem=recv_sem.at[item, slot],
            device_id={axis: peer},
            device_id_type=pl.DeviceIdType.MESH,
        )

    copies = []
    relays = []
    for item, (axis, kind) in enumerate(plan):
        size = sizes[axis]
        if kind == "relay":
            half = size // 2
            core = lax.rem(me[axis], 2)
            place = me[axis] // 2
            sibling = me[axis] + 1 - 2 * core
            for step in range(1, half):
                peer = lax.rem(place + step, half) * 2 + core
                first = copy(item, step, ins[item], outs[item].at[me[axis]], axis, peer)
                first.start()
                origin = lax.rem(place + half - step, half) * 2 + core
                relays.append((item, step, first, axis, sibling, origin))
            own = copy(item, 0, ins[item], outs[item].at[me[axis]], axis, sibling)
            own.start()
            copies.append(own)
        else:
            for step in range(1, size):
                peer = lax.rem(me[axis] + step, size)
                source = ins[item] if kind == "gather" else ins[item].at[peer]
                one = copy(item, step, source, outs[item].at[me[axis]], axis, peer)
                one.start()
                copies.append(one)
    for item, (axis, kind) in enumerate(plan):
        if kind == "swap":
            outs[item][me[axis]] = ins[item][me[axis]]
        else:
            outs[item][me[axis]] = ins[item][...]
    for item, step, first, axis, sibling, origin in relays:
        first.wait_recv()
        block = outs[item].at[origin]
        second = copy(item, sizes[axis] // 2 + step, block, block, axis, sibling)
        second.start()
        copies.append(second)
    for one in copies:
        one.wait()
    for _, _, first, _, _, _ in relays:
        first.wait_send()


def exchange(sizes, number, *items):
    plan = tuple((axis, kind) for _, axis, kind in items)
    arrays = [array for array, _, _ in items]
    shapes = []
    for array, axis, kind in items:
        shape = array.shape if kind == "swap" else (sizes[axis],) + array.shape
        shapes.append(jax.ShapeDtypeStruct(shape, array.dtype))
    slots = max(sizes[axis] for axis, _ in plan)
    vmem = pl.BlockSpec(memory_space=pltpu.VMEM)
    return pl.pallas_call(
        functools.partial(exchange_body, plan, sizes),
        out_shape=shapes,
        in_specs=[vmem] * len(arrays),
        out_specs=[vmem] * len(arrays),
        scratch_shapes=[
            pltpu.SemaphoreType.DMA((len(arrays), slots)),
            pltpu.SemaphoreType.DMA((len(arrays), slots)),
        ],
        compiler_params=pltpu.CompilerParams(collective_id=number, has_side_effects=True),
    )(*arrays)


def flat(blocks):
    return blocks.reshape((blocks.shape[0] * blocks.shape[1],) + blocks.shape[2:])


def split_body(
    sizes, hidden_in, attn_in, attn_out, fc_in, fc_out, norm_gains, biases, fc_in_bias, out_grad
):
    reps, shards = sizes["rep"], sizes["shard"]
    rank = lax.axis_index("rep")
    rows = hidden_in.shape[1]
    width = attn_out.shape[2]
    part = attn_out.shape[1]
    cols = width // reps
    units = fc_in.shape[2]
    share = units // reps
    piece = fc_out.shape[1] // reps
    heads = H // reps
    scale = (width // H) ** (-0.5)

    def mine(array, axis):
        return lax.dynamic_index_in_dim(array, rank, axis, keepdims=False)

    state = hidden_in[0].astype(F32)
    upstream = out_grad[0]
    w_in_part = mine(attn_in[0].reshape(part, 3, reps, cols), 2).reshape(part, 3 * cols)
    w_up_part = mine(fc_in[0].reshape(part, shards, reps, piece), 2).reshape(part, share)
    w_down_part = mine(fc_out[0].reshape(reps, piece, width), 0)
    small = jnp.concatenate(
        [norm_gains[0].reshape(1, -1), biases[0].reshape(1, -1), fc_in_bias[0].reshape(1, -1)], axis=1
    )
    w_out = lax.all_gather(attn_out[0], "shard", axis=0, tiled=True)
    w_up = lax.all_gather(w_up_part, "shard", axis=0, tiled=True)
    w_down = lax.all_gather(w_down_part, "shard", axis=0, tiled=True)
    w_in, small, x_all, dy_low = exchange(
        sizes,
        0,
        (w_in_part, "shard", "relay"),
        (small, "shard", "gather"),
        (hidden_in[0], "rep", "gather"),
        (upstream.astype(BF16), "rep", "gather"),
    )
    w_in, x_all, dy_low = flat(w_in), flat(x_all), flat(dy_low)
    small = small[:, 0, :].astype(F32)
    gains = small[:, : 2 * part].reshape(shards, 2, part).swapaxes(0, 1).reshape(2, width)
    shifts = small[:, 2 * part : 8 * part].reshape(shards, 6, part).swapaxes(0, 1).reshape(6, width)
    up_bias = mine(small[:, 8 * part :].reshape(shards, reps, piece), 1).reshape(share)

    normed_all, normed1_all, inv1_all = norm_forward(x_all.astype(F32), gains[0], shifts[0])
    a_low = normed_all.astype(BF16)
    _, normed1, inv1 = norm_forward(state, gains[0], shifts[0])
    qkv = jnp.dot(a_low, w_in, preferred_element_type=F32)

    def heads_of(values):
        return values.reshape(values.shape[0], heads, cols // heads)

    queries = heads_of((qkv[:, :cols] + mine(shifts[1].reshape(reps, cols), 0)).astype(BF16))
    keys = heads_of(qkv[:, cols : 2 * cols].astype(BF16))
    values_in = heads_of(
        (qkv[:, 2 * cols :] + mine(shifts[2].reshape(reps, cols), 0)).astype(BF16)
    )
    scores = jnp.einsum("qhd,khd->hqk", queries, keys, preferred_element_type=F32) * scale
    top = jnp.max(scores, axis=-1, keepdims=True)
    lse = top + jnp.log(jnp.sum(jnp.exp(scores - top), axis=-1, keepdims=True))
    probs = jnp.exp(scores - lse)
    weights = probs.astype(BF16)
    attended = jnp.einsum("hqk,khd->qhd", weights, values_in, preferred_element_type=F32)
    attended = attended.reshape(reps * rows, cols).astype(BF16)
    (o_all,) = exchange(sizes, 1, (attended, "rep", "gather"))
    o_rows = lax.dynamic_slice_in_dim(o_all, rank * rows, rows, 1)
    o_rows = o_rows.swapaxes(0, 1).reshape(rows, width)
    mixed = state + jnp.dot(o_rows, w_out, preferred_element_type=F32) + shifts[3]
    normed_mid, normed2, inv2 = norm_forward(mixed, gains[1], shifts[4])
    (c_low,) = exchange(sizes, 2, (normed_mid.astype(BF16), "rep", "gather"))
    c_low = flat(c_low)
    pre = jnp.dot(c_low, w_up, preferred_element_type=F32) + up_bias
    act_low = jax.nn.gelu(pre, approximate=False).astype(BF16)
    y_part = jnp.dot(act_low, w_down, preferred_element_type=F32).astype(BF16)

    d_down = contract_rows(act_low, dy_low)
    dpre = contract_cols(dy_low, w_down) * gelu_slope(pre)
    dpre_low = dpre.astype(BF16)
    d_up_bias = jnp.sum(dpre, axis=0)
    dmid_part = contract_cols(dpre_low, w_up).astype(BF16)
    d_up = contract_rows(c_low, dpre_low)
    ff_grads = lax.psum_scatter(
        jnp.concatenate([d_up.astype(BF16), d_down.astype(BF16)], axis=1),
        "shard",
        scatter_dimension=0,
        tiled=True,
    )
    dmid_parts, y_parts = exchange(
        sizes,
        3,
        (dmid_part.reshape(reps, rows, width), "rep", "swap"),
        (y_part.reshape(reps, rows, width), "rep", "swap"),
    )
    result = mixed + jnp.sum(y_parts.astype(F32), axis=0) + shifts[5]
    dmid = jnp.sum(dmid_parts.astype(F32), axis=0)
    de5 = jnp.sum(upstream, axis=0)
    dmixed_part, dg2, de4 = norm_backward(dmid, gains[1], normed2, inv2)
    dmixed = upstream + dmixed_part
    de3 = jnp.sum(dmixed, axis=0)
    (dmixed_low,) = exchange(sizes, 4, (dmixed.astype(BF16), "rep", "gather"))
    dmixed_low = flat(dmixed_low)
    w_out_rows = mine(w_out.reshape(reps, cols, width), 0)
    dattended = heads_of(contract_cols(dmixed_low, w_out_rows).astype(BF16))
    dmixed_cols = mine(dmixed_low.reshape(reps * rows, reps, cols), 1)
    d_out = jnp.einsum("rtc,td->rcd", o_all, dmixed_cols, preferred_element_type=F32)
    d_out = d_out.reshape(width, cols)

    dprobs = jnp.einsum("qhd,khd->hqk", dattended, values_in, preferred_element_type=F32)
    delta = jnp.sum(probs * dprobs, axis=-1, keepdims=True)
    dscores = (probs * (dprobs - delta) * scale).astype(BF16)
    dquery = jnp.einsum("hqk,khd->qhd", dscores, keys, preferred_element_type=F32)
    dkey = jnp.einsum("hqk,qhd->khd", dscores, queries, preferred_element_type=F32)
    dvalue = jnp.einsum("hqk,qhd->khd", weights, dattended, preferred_element_type=F32)
    g_qkv = jnp.stack([dquery, dkey, dvalue], axis=1).reshape(reps * rows, 3 * cols)
    de1 = jnp.sum(dquery, axis=0).reshape(cols)
    de2 = jnp.sum(dvalue, axis=0).reshape(cols)
    g_qkv = g_qkv.astype(BF16)
    dnormed_part = contract_cols(g_qkv, w_in).astype(BF16)
    d_qkv = contract_rows(a_low, g_qkv)
    attn_grads = jnp.concatenate([d_qkv.astype(BF16), d_out.astype(BF16)], axis=1)
    dnormed_parts, attn_parts = exchange(
        sizes,
        5,
        (dnormed_part.reshape(reps, rows, width), "rep", "swap"),
        (attn_grads.reshape(shards, part, width), "shard", "swap"),
    )
    attn_sum = jnp.sum(attn_parts.astype(F32), axis=0).astype(BF16)
    dnormed = jnp.sum(dnormed_parts.astype(F32), axis=0)
    dstate_part, dg1, de0 = norm_backward(dnormed, gains[0], normed1, inv1)
    dstate = dmixed + dstate_part

    def placed(values):
        spread = jnp.zeros((reps, values.shape[0]), F32)
        return lax.dynamic_update_slice_in_dim(spread, values[None], rank, 0).reshape(-1)

    full = jnp.stack([dg1, dg2, de0, placed(de1), placed(de2), de3, de4, de5])
    full = full.reshape(8, shards, part).swapaxes(0, 1).reshape(shards, 8 * part)
    bias_parts = d_up_bias.reshape(shards, 1, piece)
    bias_parts = lax.dynamic_update_slice_in_dim(
        jnp.zeros((shards, reps, piece), F32), bias_parts, rank, 1
    ).reshape(shards, reps * piece)
    vectors = jnp.concatenate([full, bias_parts], axis=1)[:, None, :]
    ff_all, attn_all, vectors = exchange(
        sizes,
        6,
        (ff_grads, "rep", "gather"),
        (attn_sum, "rep", "gather"),
        (vectors, "shard", "swap"),
    )
    (vectors,) = exchange(sizes, 7, (jnp.sum(vectors, axis=0), "rep", "gather"))
    vectors = jnp.sum(vectors, axis=0).reshape(-1)
    attn_all, ff_all = attn_all.astype(F32), ff_all.astype(F32)
    g_attn_in = attn_all[:, :, : 3 * cols].reshape(reps, part, 3, cols)
    g_attn_in = g_attn_in.transpose(1, 2, 0, 3).reshape(part, 3 * width)
    g_attn_out = attn_all[:, :, 3 * cols :].swapaxes(0, 1).reshape(part, width)
    g_fc_in = ff_all[:, :, :share].reshape(reps, part, shards, piece)
    g_fc_in = g_fc_in.transpose(1, 2, 0, 3).reshape(part, units)
    g_fc_out = ff_all[:, :, share:].reshape(reps * piece, width)
    return (
        result[None],
        dstate[None],
        g_attn_in[None],
        g_attn_out[None],
        g_fc_in[None],
        g_fc_out[None],
        vectors[: 2 * part].reshape(1, 2, part),
        vectors[2 * part : 8 * part].reshape(1, 6, part),
        vectors[8 * part :][None],
    )


def run(sizes, *args):
    reps, shards = sizes["rep"], sizes["shard"]
    width, units = args[2].shape[2], args[3].shape[2]
    even = H % reps == 0 and shards % 2 == 0 and shards > 2 and reps > 1
    if args[1].shape[0] == 1 and args[0].shape[0] == 1 and even and units % (reps * shards) == 0:
        if width // reps * reps == width:
            return split_body(sizes, *args)
    return body(*args)


def solution(mesh):
    sizes = {axis: mesh.shape[axis] for axis in ("rep", "shard")}
    in_specs = (
        P("shard", "rep", None),
        P(None, "shard", None),
        P(None, "shard", None),
        P(None, "shard", None),
        P(None, "shard", None),
        P(None, None, "shard"),
        P(None, None, "shard"),
        P(None, "shard"),
        P("shard", "rep", None),
    )
    out_specs = (
        P("shard", "rep", None),
        P("shard", "rep", None),
        P(None, "shard", None),
        P(None, "shard", None),
        P(None, "shard", None),
        P(None, "shard", None),
        P(None, None, "shard"),
        P(None, None, "shard"),
        P(None, "shard"),
    )
    return jax.shard_map(
        functools.partial(run, sizes),
        mesh=mesh,
        in_specs=in_specs,
        out_specs=out_specs,
        check_vma=False,
    )
```

```python
import functools
import math

import jax
import jax.numpy as jnp
from jax import lax
from jax.experimental import pallas as pl
from jax.experimental.pallas import tpu as pltpu
from jax.sharding import PartitionSpec as P

H = 12

BF16 = jnp.bfloat16
F32 = jnp.float32


EPS = 1e-05


def norm_forward(values, gain, shift):
    center = values - jnp.mean(values, axis=-1, keepdims=True)
    inv_root = lax.rsqrt(jnp.mean(center * center, axis=-1, keepdims=True) + EPS)
    normed = center * inv_root
    return (normed * gain + shift, normed, inv_root)


def norm_backward(upstream, gain, normed, inv_root):
    scaled = upstream * gain
    inner = (
        scaled
        - jnp.mean(scaled, axis=-1, keepdims=True)
        - normed * jnp.mean(scaled * normed, axis=-1, keepdims=True)
    )
    return (inv_root * inner, jnp.sum(upstream * normed, axis=0), jnp.sum(upstream, axis=0))


def gelu_slope(pre):
    cdf = 0.5 * (1.0 + lax.erf(pre * (1.0 / math.sqrt(2.0))))
    dens = jnp.exp(-0.5 * pre * pre) * (1.0 / math.sqrt(2.0 * math.pi))
    return cdf + pre * dens


def contract_rows(left, right):
    return lax.dot_general(
        left, right, (((0,), (0,)), ((), ())), preferred_element_type=jnp.float32
    )


def contract_cols(left, right):
    return lax.dot_general(
        left, right, (((1,), (1,)), ((), ())), preferred_element_type=jnp.float32
    )


def split_heads(values):
    return values.reshape(values.shape[0], H, values.shape[1] // H)


def score_block(queries, keys):
    scale = (queries.shape[1] // H) ** (-0.5)
    return (
        jnp.einsum(
            "qhd,khd->hqk",
            split_heads(queries),
            split_heads(keys),
            preferred_element_type=jnp.float32,
        )
        * scale
    )


def attend(queries, keys, values_in):
    scores = score_block(queries, keys)
    top = jnp.max(scores, axis=-1, keepdims=True)
    lse = top[..., 0] + jnp.log(jnp.sum(jnp.exp(scores - top), axis=-1))
    probs = jnp.exp(scores - lse[..., None]).astype(jnp.bfloat16)
    mixed = jnp.einsum(
        "hqk,khd->qhd", probs, split_heads(values_in), preferred_element_type=jnp.float32
    )
    return (mixed.reshape(queries.shape[0], -1).astype(jnp.bfloat16), lse)


def attend_back(queries, keys, values_in, lse, upstream):
    scale = (queries.shape[1] // H) ** (-0.5)
    probs = jnp.exp(score_block(queries, keys) - lse[..., None])
    weights = probs.astype(jnp.bfloat16)
    dprobs = jnp.einsum(
        "qhd,khd->hqk",
        split_heads(upstream),
        split_heads(values_in),
        preferred_element_type=jnp.float32,
    )
    delta = jnp.sum(probs * dprobs, axis=-1, keepdims=True)
    dscores = (probs * (dprobs - delta) * scale).astype(jnp.bfloat16)
    dquery = jnp.einsum(
        "hqk,khd->qhd", dscores, split_heads(keys), preferred_element_type=jnp.float32
    ).reshape(queries.shape[0], -1)
    dkey = jnp.einsum(
        "hqk,qhd->khd", dscores, split_heads(queries), preferred_element_type=jnp.float32
    ).reshape(keys.shape[0], -1)
    dvalue = jnp.einsum(
        "hqk,qhd->khd", weights, split_heads(upstream), preferred_element_type=jnp.float32
    ).reshape(keys.shape[0], -1)
    return (dquery, dkey, dvalue)


def body(hidden_in, attn_in, attn_out, fc_in, fc_out, norm_gains, biases, fc_in_bias, out_grad):
    layers = attn_in.shape[0]
    state = hidden_in[0].astype(jnp.float32)
    layer = 0
    pieces = (
        lax.all_gather(attn_in[layer], "shard", axis=0, tiled=True),
        lax.all_gather(attn_out[layer], "shard", axis=0, tiled=True),
        lax.all_gather(fc_in[layer], "shard", axis=0, tiled=True),
        lax.all_gather(fc_out[layer], "shard", axis=0, tiled=True),
        lax.all_gather(norm_gains[layer], "shard", axis=1, tiled=True),
        lax.all_gather(biases[layer], "shard", axis=1, tiled=True),
        lax.all_gather(fc_in_bias[layer], "shard", axis=0, tiled=True),
    )
    w_qkv = pieces[0]
    w_out = pieces[1]
    w_up = pieces[2]
    w_down = pieces[3]
    gains = pieces[4].astype(jnp.float32)
    shifts = pieces[5].astype(jnp.float32)
    up_bias = pieces[6].astype(jnp.float32)
    width = w_out.shape[0]
    normed_in, normed1, inv1 = norm_forward(state, gains[0], shifts[0])
    a_low = normed_in.astype(jnp.bfloat16)
    qkv = jnp.dot(a_low, w_qkv, preferred_element_type=jnp.float32)
    queries = (qkv[:, :width] + shifts[1]).astype(jnp.bfloat16)
    keys_local = qkv[:, width : 2 * width].astype(jnp.bfloat16)
    values_local = (qkv[:, 2 * width :] + shifts[2]).astype(jnp.bfloat16)
    keys_all = lax.all_gather(keys_local, "rep", axis=0, tiled=True)
    values_all = lax.all_gather(values_local, "rep", axis=0, tiled=True)
    attended, lse = attend(queries, keys_all, values_all)
    mixed = state + jnp.dot(attended, w_out, preferred_element_type=jnp.float32) + shifts[3]
    normed_mid, normed2, inv2 = norm_forward(mixed, gains[1], shifts[4])
    c_low = normed_mid.astype(jnp.bfloat16)
    pre = jnp.dot(c_low, w_up, preferred_element_type=jnp.float32) + up_bias
    act_low = jax.nn.gelu(pre, approximate=False).astype(jnp.bfloat16)
    result = mixed + jnp.dot(act_low, w_down, preferred_element_type=jnp.float32) + shifts[5]
    saved = [
        (
            normed1,
            inv1,
            a_low,
            queries,
            keys_all,
            values_all,
            lse,
            attended,
            normed2,
            inv2,
            c_low,
            pre,
            act_low,
            (w_qkv, w_out, w_up, w_down, gains),
        )
    ]
    upstream = out_grad[0]
    layer_grads = [None] * layers
    for layer in reversed(range(layers)):
        (
            normed1,
            inv1,
            a_low,
            queries,
            keys_all,
            values_all,
            lse,
            attended,
            normed2,
            inv2,
            c_low,
            pre,
            act_low,
            held,
        ) = saved[layer]
        w_qkv, w_out, w_up, w_down, gains = held
        dy_low = upstream.astype(jnp.bfloat16)
        d_down = contract_rows(act_low, dy_low)
        de5 = jnp.sum(upstream, axis=0)
        dact = contract_cols(dy_low, w_down)
        dpre = dact * gelu_slope(pre)
        dpre_low = dpre.astype(jnp.bfloat16)
        d_up = contract_rows(c_low, dpre_low)
        d_up_bias = jnp.sum(dpre, axis=0)
        dmid = contract_cols(dpre_low, w_up)
        dmixed_part, dg2, de4 = norm_backward(dmid, gains[1], normed2, inv2)
        dmixed = upstream + dmixed_part
        dmixed_low = dmixed.astype(jnp.bfloat16)
        d_out = contract_rows(attended, dmixed_low)
        de3 = jnp.sum(dmixed, axis=0)
        dattended = contract_cols(dmixed_low, w_out).astype(jnp.bfloat16)
        dquery, dkey_part, dvalue_part = attend_back(queries, keys_all, values_all, lse, dattended)
        dkey, dvalue = (
            lax.psum_scatter(
                dkey_part.astype(jnp.bfloat16), "rep", scatter_dimension=0, tiled=True
            ).astype(jnp.float32),
            lax.psum_scatter(
                dvalue_part.astype(jnp.bfloat16), "rep", scatter_dimension=0, tiled=True
            ).astype(jnp.float32),
        )
        g_qkv = jnp.concatenate([dquery, dkey, dvalue], axis=1).astype(jnp.bfloat16)
        d_qkv = contract_rows(a_low, g_qkv)
        de1 = jnp.sum(dquery, axis=0)
        de2 = jnp.sum(dvalue, axis=0)
        dnormed = contract_cols(g_qkv, w_qkv)
        dstate_part, dg1, de0 = norm_backward(dnormed, gains[0], normed1, inv1)
        upstream = dmixed + dstate_part
        owned = (
            lax.psum_scatter(
                d_qkv.astype(jnp.bfloat16), "shard", scatter_dimension=0, tiled=True
            ).astype(jnp.float32),
            lax.psum_scatter(
                d_out.astype(jnp.bfloat16), "shard", scatter_dimension=0, tiled=True
            ).astype(jnp.float32),
            lax.psum_scatter(
                d_up.astype(jnp.bfloat16), "shard", scatter_dimension=0, tiled=True
            ).astype(jnp.float32),
            lax.psum_scatter(
                d_down.astype(jnp.bfloat16), "shard", scatter_dimension=0, tiled=True
            ).astype(jnp.float32),
            lax.psum_scatter(
                jnp.stack([dg1, dg2]).astype(jnp.bfloat16), "shard", scatter_dimension=1, tiled=True
            ).astype(jnp.float32),
            lax.psum_scatter(
                jnp.stack([de0, de1, de2, de3, de4, de5]).astype(jnp.bfloat16),
                "shard",
                scatter_dimension=1,
                tiled=True,
            ).astype(jnp.float32),
            lax.psum_scatter(
                d_up_bias.astype(jnp.bfloat16), "shard", scatter_dimension=0, tiled=True
            ).astype(jnp.float32),
        )
        owned = (
            lax.psum(owned[0].astype(jnp.bfloat16), "rep").astype(jnp.float32),
            lax.psum(owned[1].astype(jnp.bfloat16), "rep").astype(jnp.float32),
            lax.psum(owned[2].astype(jnp.bfloat16), "rep").astype(jnp.float32),
            lax.psum(owned[3].astype(jnp.bfloat16), "rep").astype(jnp.float32),
            lax.psum(owned[4].astype(jnp.bfloat16), "rep").astype(jnp.float32),
            lax.psum(owned[5].astype(jnp.bfloat16), "rep").astype(jnp.float32),
            lax.psum(owned[6].astype(jnp.bfloat16), "rep").astype(jnp.float32),
        )
        layer_grads[layer] = owned
    stacked = tuple((jnp.stack([grads[index] for grads in layer_grads]) for index in range(7)))
    return (
        result[None],
        upstream[None],
        stacked[0],
        stacked[1],
        stacked[2],
        stacked[3],
        stacked[4],
        stacked[5],
        stacked[6],
    )


def exchange_body(plan, sizes, *refs):
    count = len(plan)
    ins, outs = refs[:count], refs[count : 2 * count]
    send_sem, recv_sem = refs[2 * count :]
    me = {axis: lax.axis_index(axis) for axis in sizes}
    barrier = pltpu.get_barrier_semaphore()
    greeted = 0
    offsets = set()
    for axis, kind in plan:
        for rep_step in range(sizes["rep"]):
            for shard_step in range(sizes["shard"]):
                along = (shard_step if axis == "rep" else rep_step) == 0
                if (along or kind == "spread") and (rep_step, shard_step) != (0, 0):
                    offsets.add((rep_step, shard_step))

    def at(rep_step, shard_step):
        return {
            "rep": lax.rem(me["rep"] + rep_step, sizes["rep"]),
            "shard": lax.rem(me["shard"] + shard_step, sizes["shard"]),
        }

    for offset in sorted(offsets):
        pl.semaphore_signal(
            barrier, inc=1, device_id=at(*offset), device_id_type=pl.DeviceIdType.MESH
        )
        greeted += 1
    pl.semaphore_wait(barrier, greeted)

    def copy(item, slot, source, target, axis, peer):
        return pltpu.make_async_remote_copy(
            src_ref=source,
            dst_ref=target,
            send_sem=send_sem.at[item, slot],
            recv_sem=recv_sem.at[item, slot],
            device_id=peer if axis is None else {axis: peer},
            device_id_type=pl.DeviceIdType.MESH,
        )

    copies = []
    relays = []
    for item, (axis, kind) in enumerate(plan):
        size = sizes[axis]
        if kind == "relay":
            half = size // 2
            core = lax.rem(me[axis], 2)
            place = me[axis] // 2
            sibling = me[axis] + 1 - 2 * core
            for step in range(1, half):
                peer = lax.rem(place + step, half) * 2 + core
                first = copy(item, step, ins[item], outs[item].at[me[axis]], axis, peer)
                first.start()
                origin = lax.rem(place + half - step, half) * 2 + core
                relays.append((item, step, first, axis, sibling, origin))
            own = copy(item, 0, ins[item], outs[item].at[me[axis]], axis, sibling)
            own.start()
            copies.append(own)
        elif kind == "spread":
            for rep_step in range(sizes["rep"]):
                for shard_step in range(sizes["shard"]):
                    if (rep_step, shard_step) != (0, 0):
                        peer = at(rep_step, shard_step)
                        target = outs[item].at[me["rep"], me["shard"]]
                        slot = rep_step * sizes["shard"] + shard_step
                        one = copy(item, slot, ins[item].at[peer["shard"]], target, None, peer)
                        one.start()
                        copies.append(one)
        else:
            for step in range(1, size):
                peer = lax.rem(me[axis] + step, size)
                source = ins[item] if kind == "gather" else ins[item].at[peer]
                one = copy(item, step, source, outs[item].at[me[axis]], axis, peer)
                one.start()
                copies.append(one)
    for item, (axis, kind) in enumerate(plan):
        if kind == "swap":
            outs[item][me[axis]] = ins[item][me[axis]]
        elif kind == "spread":
            outs[item][me["rep"], me["shard"]] = ins[item][me["shard"]]
        else:
            outs[item][me[axis]] = ins[item][...]
    for item, step, first, axis, sibling, origin in relays:
        first.wait_recv()
        block = outs[item].at[origin]
        second = copy(item, sizes[axis] // 2 + step, block, block, axis, sibling)
        second.start()
        copies.append(second)
    for one in copies:
        one.wait()
    for _, _, first, _, _, _ in relays:
        first.wait_send()


def exchange(sizes, number, *items):
    plan = tuple((axis, kind) for _, axis, kind in items)
    arrays = [array for array, _, _ in items]
    shapes = []
    for array, axis, kind in items:
        shape = array.shape if kind == "swap" else (sizes[axis],) + array.shape
        if kind == "spread":
            shape = (sizes["rep"],) + array.shape
        shapes.append(jax.ShapeDtypeStruct(shape, array.dtype))
    slots = max(sizes[axis] for axis, _ in plan)
    if any(kind == "spread" for _, kind in plan):
        slots = sizes["rep"] * sizes["shard"]
    vmem = pl.BlockSpec(memory_space=pltpu.VMEM)
    return pl.pallas_call(
        functools.partial(exchange_body, plan, sizes),
        out_shape=shapes,
        in_specs=[vmem] * len(arrays),
        out_specs=[vmem] * len(arrays),
        scratch_shapes=[
            pltpu.SemaphoreType.DMA((len(arrays), slots)),
            pltpu.SemaphoreType.DMA((len(arrays), slots)),
        ],
        compiler_params=pltpu.CompilerParams(collective_id=number, has_side_effects=True),
    )(*arrays)


def local(kernel, shapes, *arrays):
    vmem = pl.BlockSpec(memory_space=pltpu.VMEM)
    return pl.pallas_call(
        kernel,
        out_shape=shapes,
        in_specs=[vmem] * len(arrays),
        out_specs=[vmem] * len(shapes),
    )(*arrays)


def prepare_kernel(reps, shards, attn_in, fc_in, fc_out, w_in, w_ff):
    rank = lax.axis_index("rep")
    cols = w_in.shape[1] // 3
    piece = fc_out.shape[0] // reps
    width = cols * reps
    share = shards * piece
    for r in range(reps):

        @pl.when(rank == r)
        def _(r=r):
            for k in range(3):
                base = k * width + r * cols
                w_in[:, k * cols : (k + 1) * cols] = attn_in[:, base : base + cols]
            for k in range(shards):
                base = (k * reps + r) * piece
                w_ff[:, k * piece : (k + 1) * piece] = fc_in[:, base : base + piece]
            w_ff[:, share:] = fc_out[r * piece : (r + 1) * piece, :]


def finish_kernel(reps, shards, attn_all, ff_all, attn_in, attn_out, fc_in, fc_out):
    width = attn_out.shape[1]
    cols = width // reps
    piece = fc_out.shape[0] // reps
    share = shards * piece
    for r in range(reps):
        for k in range(3):
            base = k * width + r * cols
            attn_in[:, base : base + cols] = attn_all[r, :, k * cols : (k + 1) * cols].astype(F32)
        attn_out[:, r * cols : (r + 1) * cols] = attn_all[r, :, 3 * cols :].astype(F32)
        for k in range(shards):
            base = (k * reps + r) * piece
            fc_in[:, base : base + piece] = ff_all[r, :, k * piece : (k + 1) * piece].astype(F32)
        fc_out[r * piece : (r + 1) * piece, :] = ff_all[r, :, share:].astype(F32)


def attend_kernel(heads, qkv, mixed, lse):
    cols = mixed.shape[1]
    depth = cols // heads
    scale = depth ** (-0.5)
    for h in range(heads):
        here = slice(h * depth, (h + 1) * depth)
        query = qkv[:, h * depth : (h + 1) * depth]
        key = qkv[:, cols + h * depth : cols + (h + 1) * depth]
        value = qkv[:, 2 * cols + h * depth : 2 * cols + (h + 1) * depth]
        scores = contract_cols(query, key) * scale
        top = jnp.max(scores, axis=-1, keepdims=True)
        total = top + jnp.log(jnp.sum(jnp.exp(scores - top), axis=-1, keepdims=True))
        probs = jnp.exp(scores - total).astype(BF16)
        mixed[:, here] = jnp.dot(probs, value, preferred_element_type=F32).astype(BF16)
        lse[:, h : h + 1] = total


def attend_back_kernel(heads, qkv, upstream, lse, grad, query_sum, value_sum):
    cols = upstream.shape[1]
    depth = cols // heads
    scale = depth ** (-0.5)
    for h in range(heads):
        first = slice(h * depth, (h + 1) * depth)
        second = slice(cols + h * depth, cols + (h + 1) * depth)
        third = slice(2 * cols + h * depth, 2 * cols + (h + 1) * depth)
        query, key, value, above = qkv[:, first], qkv[:, second], qkv[:, third], upstream[:, first]
        probs = jnp.exp(contract_cols(query, key) * scale - lse[:, h : h + 1])
        dprobs = contract_cols(above, value)
        delta = jnp.sum(probs * dprobs, axis=-1, keepdims=True)
        dscores = (probs * (dprobs - delta) * scale).astype(BF16)
        dquery = jnp.dot(dscores, key, preferred_element_type=F32)
        dvalue = contract_rows(probs.astype(BF16), above)
        grad[:, first] = dquery.astype(BF16)
        grad[:, second] = contract_rows(dscores, query).astype(BF16)
        grad[:, third] = dvalue.astype(BF16)
        query_sum[:, first] = jnp.sum(dquery, axis=0, keepdims=True)
        value_sum[:, first] = jnp.sum(dvalue, axis=0, keepdims=True)


def flat(blocks):
    return blocks.reshape((blocks.shape[0] * blocks.shape[1],) + blocks.shape[2:])


def split_body(
    sizes, hidden_in, attn_in, attn_out, fc_in, fc_out, norm_gains, biases, fc_in_bias, out_grad
):
    reps, shards = sizes["rep"], sizes["shard"]
    rank = lax.axis_index("rep")
    rows = hidden_in.shape[1]
    width = attn_out.shape[2]
    part = attn_out.shape[1]
    cols = width // reps
    units = fc_in.shape[2]
    share = units // reps
    piece = fc_out.shape[1] // reps
    heads = H // reps

    def mine(array, axis):
        return lax.dynamic_index_in_dim(array, rank, axis, keepdims=False)

    state = hidden_in[0].astype(F32)
    upstream = out_grad[0]
    w_in_part, w_ff_part = local(
        functools.partial(prepare_kernel, reps, shards),
        [
            jax.ShapeDtypeStruct((part, 3 * cols), BF16),
            jax.ShapeDtypeStruct((part, share + width), BF16),
        ],
        attn_in[0],
        fc_in[0],
        fc_out[0],
    )
    small = jnp.concatenate(
        [norm_gains[0].reshape(1, -1), biases[0].reshape(1, -1), fc_in_bias[0].reshape(1, -1)], axis=1
    )
    w_in, w_out, small, x_all, dy_low = exchange(
        sizes,
        0,
        (w_in_part, "shard", "relay"),
        (attn_out[0], "shard", "relay"),
        (small, "shard", "gather"),
        (hidden_in[0], "rep", "gather"),
        (upstream.astype(BF16), "rep", "gather"),
    )
    w_ff_part, w_in = lax.optimization_barrier((w_ff_part, w_in))
    w_ff = lax.all_gather(w_ff_part, "shard", axis=0, tiled=True)
    w_up, w_down = w_ff[:, :share], w_ff[:, share:]
    w_in, w_out, x_all, dy_low = flat(w_in), flat(w_out), flat(x_all), flat(dy_low)
    small = small[:, 0, :].astype(F32)
    gains = small[:, : 2 * part].reshape(shards, 2, part).swapaxes(0, 1).reshape(2, width)
    shifts = small[:, 2 * part : 8 * part].reshape(shards, 6, part).swapaxes(0, 1).reshape(6, width)
    up_bias = mine(small[:, 8 * part :].reshape(shards, reps, piece), 1).reshape(share)

    normed_all, normed1_all, inv1_all = norm_forward(x_all.astype(F32), gains[0], shifts[0])
    a_low = normed_all.astype(BF16)
    _, normed1, inv1 = norm_forward(state, gains[0], shifts[0])
    qkv = jnp.dot(a_low, w_in, preferred_element_type=F32)
    query_bias = mine(shifts[1].reshape(reps, cols), 0)
    value_bias = mine(shifts[2].reshape(reps, cols), 0)
    qkv = qkv + jnp.concatenate([query_bias, jnp.zeros_like(query_bias), value_bias])
    qkv = qkv.astype(BF16)
    attended, lse = local(
        functools.partial(attend_kernel, heads),
        [
            jax.ShapeDtypeStruct((reps * rows, cols), BF16),
            jax.ShapeDtypeStruct((reps * rows, heads), F32),
        ],
        qkv,
    )
    (o_all,) = exchange(sizes, 1, (attended, "rep", "gather"))
    o_rows = lax.dynamic_slice_in_dim(o_all, rank * rows, rows, 1)
    o_rows = o_rows.swapaxes(0, 1).reshape(rows, width)
    mixed = state + jnp.dot(o_rows, w_out, preferred_element_type=F32) + shifts[3]
    normed_mid, normed2, inv2 = norm_forward(mixed, gains[1], shifts[4])
    (c_low,) = exchange(sizes, 2, (normed_mid.astype(BF16), "rep", "gather"))
    c_low = flat(c_low)
    pre = jnp.dot(c_low, w_up, preferred_element_type=F32) + up_bias
    act_low = jax.nn.gelu(pre, approximate=False).astype(BF16)
    y_part = jnp.dot(act_low, w_down, preferred_element_type=F32).astype(BF16)

    d_down = contract_rows(act_low, dy_low)
    dpre = contract_cols(dy_low, w_down) * gelu_slope(pre)
    dpre_low = dpre.astype(BF16)
    d_up_bias = jnp.sum(dpre, axis=0)
    dmid_part = contract_cols(dpre_low, w_up).astype(BF16)
    d_up = contract_rows(c_low, dpre_low)
    ff_grads = lax.psum_scatter(
        jnp.concatenate([d_up.astype(BF16), d_down.astype(BF16)], axis=1),
        "shard",
        scatter_dimension=0,
        tiled=True,
    )
    (dmid_parts,) = exchange(sizes, 3, (dmid_part.reshape(reps, rows, width), "rep", "swap"))
    dmid = jnp.sum(dmid_parts.astype(F32), axis=0)
    de5 = jnp.sum(upstream, axis=0)
    dmixed_part, dg2, de4 = norm_backward(dmid, gains[1], normed2, inv2)
    dmixed = upstream + dmixed_part
    de3 = jnp.sum(dmixed, axis=0)
    (dmixed_low,) = exchange(sizes, 4, (dmixed.astype(BF16), "rep", "gather"))
    dmixed_low = flat(dmixed_low)
    w_out_rows = mine(w_out.reshape(reps, cols, width), 0)
    dattended = contract_cols(dmixed_low, w_out_rows).astype(BF16)
    dmixed_cols = mine(dmixed_low.reshape(reps * rows, reps, cols), 1)
    d_out = jnp.einsum("rtc,td->rcd", o_all, dmixed_cols, preferred_element_type=F32)
    d_out = d_out.reshape(width, cols)

    g_qkv, de1, de2 = local(
        functools.partial(attend_back_kernel, heads),
        [
            jax.ShapeDtypeStruct((reps * rows, 3 * cols), BF16),
            jax.ShapeDtypeStruct((1, cols), F32),
            jax.ShapeDtypeStruct((1, cols), F32),
        ],
        qkv,
        dattended,
        lse,
    )
    de1, de2 = de1[0], de2[0]
    dnormed_part = contract_cols(g_qkv, w_in).astype(BF16)
    d_qkv = contract_rows(a_low, g_qkv)
    attn_grads = jnp.concatenate([d_qkv.astype(BF16), d_out.astype(BF16)], axis=1)
    dnormed_parts, y_parts, ff_all, attn_parts = exchange(
        sizes,
        5,
        (dnormed_part.reshape(reps, rows, width), "rep", "swap"),
        (y_part.reshape(reps, rows, width), "rep", "swap"),
        (ff_grads, "rep", "gather"),
        (attn_grads.reshape(shards, part, width), "shard", "swap"),
    )
    result = mixed + jnp.sum(y_parts.astype(F32), axis=0) + shifts[5]
    attn_sum = jnp.sum(attn_parts.astype(F32), axis=0).astype(BF16)
    dnormed = jnp.sum(dnormed_parts.astype(F32), axis=0)
    dstate_part, dg1, de0 = norm_backward(dnormed, gains[0], normed1, inv1)
    dstate = dmixed + dstate_part

    def placed(values):
        spread = jnp.zeros((reps, values.shape[0]), F32)
        return lax.dynamic_update_slice_in_dim(spread, values[None], rank, 0).reshape(-1)

    full = jnp.stack([dg1, dg2, de0, placed(de1), placed(de2), de3, de4, de5])
    full = full.reshape(8, shards, part).swapaxes(0, 1).reshape(shards, 8 * part)
    bias_parts = d_up_bias.reshape(shards, 1, piece)
    bias_parts = lax.dynamic_update_slice_in_dim(
        jnp.zeros((shards, reps, piece), F32), bias_parts, rank, 1
    ).reshape(shards, reps * piece)
    vectors = jnp.concatenate([full, bias_parts], axis=1)[:, None, :]
    attn_all, vectors = exchange(
        sizes, 6, (attn_sum, "rep", "gather"), (vectors, "shard", "spread")
    )
    vectors = jnp.sum(vectors, axis=(0, 1)).reshape(-1)
    g_attn_in, g_attn_out, g_fc_in, g_fc_out = local(
        functools.partial(finish_kernel, reps, shards),
        [
            jax.ShapeDtypeStruct((part, 3 * width), F32),
            jax.ShapeDtypeStruct((part, width), F32),
            jax.ShapeDtypeStruct((part, units), F32),
            jax.ShapeDtypeStruct((reps * piece, width), F32),
        ],
        attn_all,
        ff_all,
    )
    return (
        result[None],
        dstate[None],
        g_attn_in[None],
        g_attn_out[None],
        g_fc_in[None],
        g_fc_out[None],
        vectors[: 2 * part].reshape(1, 2, part),
        vectors[2 * part : 8 * part].reshape(1, 6, part),
        vectors[8 * part :][None],
    )


def run(sizes, *args):
    reps, shards = sizes["rep"], sizes["shard"]
    width, units = args[2].shape[2], args[3].shape[2]
    even = H % reps == 0 and shards % 2 == 0 and shards > 2 and reps > 1
    if args[1].shape[0] == 1 and args[0].shape[0] == 1 and even and units % (reps * shards) == 0:
        if width // reps * reps == width:
            return split_body(sizes, *args)
    return body(*args)


def solution(mesh):
    sizes = {axis: mesh.shape[axis] for axis in ("rep", "shard")}
    in_specs = (
        P("shard", "rep", None),
        P(None, "shard", None),
        P(None, "shard", None),
        P(None, "shard", None),
        P(None, "shard", None),
        P(None, None, "shard"),
        P(None, None, "shard"),
        P(None, "shard"),
        P("shard", "rep", None),
    )
    out_specs = (
        P("shard", "rep", None),
        P("shard", "rep", None),
        P(None, "shard", None),
        P(None, "shard", None),
        P(None, "shard", None),
        P(None, "shard", None),
        P(None, None, "shard"),
        P(None, None, "shard"),
        P(None, "shard"),
    )
    return jax.shard_map(
        functools.partial(run, sizes),
        mesh=mesh,
        in_specs=in_specs,
        out_specs=out_specs,
        check_vma=False,
    )
```

```python
import functools
import math

import jax
import jax.numpy as jnp
from jax import lax
from jax.experimental import pallas as pl
from jax.experimental.pallas import tpu as pltpu
from jax.sharding import PartitionSpec as P

H = 12

BF16 = jnp.bfloat16
F32 = jnp.float32


EPS = 1e-05


def norm_forward(values, gain, shift):
    center = values - jnp.mean(values, axis=-1, keepdims=True)
    inv_root = lax.rsqrt(jnp.mean(center * center, axis=-1, keepdims=True) + EPS)
    normed = center * inv_root
    return (normed * gain + shift, normed, inv_root)


def norm_backward(upstream, gain, normed, inv_root):
    scaled = upstream * gain
    inner = (
        scaled
        - jnp.mean(scaled, axis=-1, keepdims=True)
        - normed * jnp.mean(scaled * normed, axis=-1, keepdims=True)
    )
    return (inv_root * inner, jnp.sum(upstream * normed, axis=0), jnp.sum(upstream, axis=0))


def gelu_slope(pre):
    cdf = 0.5 * (1.0 + lax.erf(pre * (1.0 / math.sqrt(2.0))))
    dens = jnp.exp(-0.5 * pre * pre) * (1.0 / math.sqrt(2.0 * math.pi))
    return cdf + pre * dens


def contract_rows(left, right):
    return lax.dot_general(
        left, right, (((0,), (0,)), ((), ())), preferred_element_type=jnp.float32
    )


def contract_cols(left, right):
    return lax.dot_general(
        left, right, (((1,), (1,)), ((), ())), preferred_element_type=jnp.float32
    )


def split_heads(values):
    return values.reshape(values.shape[0], H, values.shape[1] // H)


def score_block(queries, keys):
    scale = (queries.shape[1] // H) ** (-0.5)
    return (
        jnp.einsum(
            "qhd,khd->hqk",
            split_heads(queries),
            split_heads(keys),
            preferred_element_type=jnp.float32,
        )
        * scale
    )


def attend(queries, keys, values_in):
    scores = score_block(queries, keys)
    top = jnp.max(scores, axis=-1, keepdims=True)
    lse = top[..., 0] + jnp.log(jnp.sum(jnp.exp(scores - top), axis=-1))
    probs = jnp.exp(scores - lse[..., None]).astype(jnp.bfloat16)
    mixed = jnp.einsum(
        "hqk,khd->qhd", probs, split_heads(values_in), preferred_element_type=jnp.float32
    )
    return (mixed.reshape(queries.shape[0], -1).astype(jnp.bfloat16), lse)


def attend_back(queries, keys, values_in, lse, upstream):
    scale = (queries.shape[1] // H) ** (-0.5)
    probs = jnp.exp(score_block(queries, keys) - lse[..., None])
    weights = probs.astype(jnp.bfloat16)
    dprobs = jnp.einsum(
        "qhd,khd->hqk",
        split_heads(upstream),
        split_heads(values_in),
        preferred_element_type=jnp.float32,
    )
    delta = jnp.sum(probs * dprobs, axis=-1, keepdims=True)
    dscores = (probs * (dprobs - delta) * scale).astype(jnp.bfloat16)
    dquery = jnp.einsum(
        "hqk,khd->qhd", dscores, split_heads(keys), preferred_element_type=jnp.float32
    ).reshape(queries.shape[0], -1)
    dkey = jnp.einsum(
        "hqk,qhd->khd", dscores, split_heads(queries), preferred_element_type=jnp.float32
    ).reshape(keys.shape[0], -1)
    dvalue = jnp.einsum(
        "hqk,qhd->khd", weights, split_heads(upstream), preferred_element_type=jnp.float32
    ).reshape(keys.shape[0], -1)
    return (dquery, dkey, dvalue)


def body(hidden_in, attn_in, attn_out, fc_in, fc_out, norm_gains, biases, fc_in_bias, out_grad):
    layers = attn_in.shape[0]
    state = hidden_in[0].astype(jnp.float32)
    layer = 0
    pieces = (
        lax.all_gather(attn_in[layer], "shard", axis=0, tiled=True),
        lax.all_gather(attn_out[layer], "shard", axis=0, tiled=True),
        lax.all_gather(fc_in[layer], "shard", axis=0, tiled=True),
        lax.all_gather(fc_out[layer], "shard", axis=0, tiled=True),
        lax.all_gather(norm_gains[layer], "shard", axis=1, tiled=True),
        lax.all_gather(biases[layer], "shard", axis=1, tiled=True),
        lax.all_gather(fc_in_bias[layer], "shard", axis=0, tiled=True),
    )
    w_qkv = pieces[0]
    w_out = pieces[1]
    w_up = pieces[2]
    w_down = pieces[3]
    gains = pieces[4].astype(jnp.float32)
    shifts = pieces[5].astype(jnp.float32)
    up_bias = pieces[6].astype(jnp.float32)
    width = w_out.shape[0]
    normed_in, normed1, inv1 = norm_forward(state, gains[0], shifts[0])
    a_low = normed_in.astype(jnp.bfloat16)
    qkv = jnp.dot(a_low, w_qkv, preferred_element_type=jnp.float32)
    queries = (qkv[:, :width] + shifts[1]).astype(jnp.bfloat16)
    keys_local = qkv[:, width : 2 * width].astype(jnp.bfloat16)
    values_local = (qkv[:, 2 * width :] + shifts[2]).astype(jnp.bfloat16)
    keys_all = lax.all_gather(keys_local, "rep", axis=0, tiled=True)
    values_all = lax.all_gather(values_local, "rep", axis=0, tiled=True)
    attended, lse = attend(queries, keys_all, values_all)
    mixed = state + jnp.dot(attended, w_out, preferred_element_type=jnp.float32) + shifts[3]
    normed_mid, normed2, inv2 = norm_forward(mixed, gains[1], shifts[4])
    c_low = normed_mid.astype(jnp.bfloat16)
    pre = jnp.dot(c_low, w_up, preferred_element_type=jnp.float32) + up_bias
    act_low = jax.nn.gelu(pre, approximate=False).astype(jnp.bfloat16)
    result = mixed + jnp.dot(act_low, w_down, preferred_element_type=jnp.float32) + shifts[5]
    saved = [
        (
            normed1,
            inv1,
            a_low,
            queries,
            keys_all,
            values_all,
            lse,
            attended,
            normed2,
            inv2,
            c_low,
            pre,
            act_low,
            (w_qkv, w_out, w_up, w_down, gains),
        )
    ]
    upstream = out_grad[0]
    layer_grads = [None] * layers
    for layer in reversed(range(layers)):
        (
            normed1,
            inv1,
            a_low,
            queries,
            keys_all,
            values_all,
            lse,
            attended,
            normed2,
            inv2,
            c_low,
            pre,
            act_low,
            held,
        ) = saved[layer]
        w_qkv, w_out, w_up, w_down, gains = held
        dy_low = upstream.astype(jnp.bfloat16)
        d_down = contract_rows(act_low, dy_low)
        de5 = jnp.sum(upstream, axis=0)
        dact = contract_cols(dy_low, w_down)
        dpre = dact * gelu_slope(pre)
        dpre_low = dpre.astype(jnp.bfloat16)
        d_up = contract_rows(c_low, dpre_low)
        d_up_bias = jnp.sum(dpre, axis=0)
        dmid = contract_cols(dpre_low, w_up)
        dmixed_part, dg2, de4 = norm_backward(dmid, gains[1], normed2, inv2)
        dmixed = upstream + dmixed_part
        dmixed_low = dmixed.astype(jnp.bfloat16)
        d_out = contract_rows(attended, dmixed_low)
        de3 = jnp.sum(dmixed, axis=0)
        dattended = contract_cols(dmixed_low, w_out).astype(jnp.bfloat16)
        dquery, dkey_part, dvalue_part = attend_back(queries, keys_all, values_all, lse, dattended)
        dkey, dvalue = (
            lax.psum_scatter(
                dkey_part.astype(jnp.bfloat16), "rep", scatter_dimension=0, tiled=True
            ).astype(jnp.float32),
            lax.psum_scatter(
                dvalue_part.astype(jnp.bfloat16), "rep", scatter_dimension=0, tiled=True
            ).astype(jnp.float32),
        )
        g_qkv = jnp.concatenate([dquery, dkey, dvalue], axis=1).astype(jnp.bfloat16)
        d_qkv = contract_rows(a_low, g_qkv)
        de1 = jnp.sum(dquery, axis=0)
        de2 = jnp.sum(dvalue, axis=0)
        dnormed = contract_cols(g_qkv, w_qkv)
        dstate_part, dg1, de0 = norm_backward(dnormed, gains[0], normed1, inv1)
        upstream = dmixed + dstate_part
        owned = (
            lax.psum_scatter(
                d_qkv.astype(jnp.bfloat16), "shard", scatter_dimension=0, tiled=True
            ).astype(jnp.float32),
            lax.psum_scatter(
                d_out.astype(jnp.bfloat16), "shard", scatter_dimension=0, tiled=True
            ).astype(jnp.float32),
            lax.psum_scatter(
                d_up.astype(jnp.bfloat16), "shard", scatter_dimension=0, tiled=True
            ).astype(jnp.float32),
            lax.psum_scatter(
                d_down.astype(jnp.bfloat16), "shard", scatter_dimension=0, tiled=True
            ).astype(jnp.float32),
            lax.psum_scatter(
                jnp.stack([dg1, dg2]).astype(jnp.bfloat16), "shard", scatter_dimension=1, tiled=True
            ).astype(jnp.float32),
            lax.psum_scatter(
                jnp.stack([de0, de1, de2, de3, de4, de5]).astype(jnp.bfloat16),
                "shard",
                scatter_dimension=1,
                tiled=True,
            ).astype(jnp.float32),
            lax.psum_scatter(
                d_up_bias.astype(jnp.bfloat16), "shard", scatter_dimension=0, tiled=True
            ).astype(jnp.float32),
        )
        owned = (
            lax.psum(owned[0].astype(jnp.bfloat16), "rep").astype(jnp.float32),
            lax.psum(owned[1].astype(jnp.bfloat16), "rep").astype(jnp.float32),
            lax.psum(owned[2].astype(jnp.bfloat16), "rep").astype(jnp.float32),
            lax.psum(owned[3].astype(jnp.bfloat16), "rep").astype(jnp.float32),
            lax.psum(owned[4].astype(jnp.bfloat16), "rep").astype(jnp.float32),
            lax.psum(owned[5].astype(jnp.bfloat16), "rep").astype(jnp.float32),
            lax.psum(owned[6].astype(jnp.bfloat16), "rep").astype(jnp.float32),
        )
        layer_grads[layer] = owned
    stacked = tuple((jnp.stack([grads[index] for grads in layer_grads]) for index in range(7)))
    return (
        result[None],
        upstream[None],
        stacked[0],
        stacked[1],
        stacked[2],
        stacked[3],
        stacked[4],
        stacked[5],
        stacked[6],
    )


def exchange_body(plan, sizes, *refs):
    count = len(plan)
    ins, outs = refs[:count], refs[count : 2 * count]
    send_sem, recv_sem = refs[2 * count :]
    me = {axis: lax.axis_index(axis) for axis in sizes}
    barrier = pltpu.get_barrier_semaphore()
    greeted = 0
    offsets = set()
    for axis, kind in plan:
        for rep_step in range(sizes["rep"]):
            for shard_step in range(sizes["shard"]):
                along = (shard_step if axis == "rep" else rep_step) == 0
                if (along or kind == "spread") and (rep_step, shard_step) != (0, 0):
                    offsets.add((rep_step, shard_step))

    def at(rep_step, shard_step):
        return {
            "rep": lax.rem(me["rep"] + rep_step, sizes["rep"]),
            "shard": lax.rem(me["shard"] + shard_step, sizes["shard"]),
        }

    for offset in sorted(offsets):
        pl.semaphore_signal(
            barrier, inc=1, device_id=at(*offset), device_id_type=pl.DeviceIdType.MESH
        )
        greeted += 1
    pl.semaphore_wait(barrier, greeted)

    def copy(item, slot, source, target, axis, peer):
        return pltpu.make_async_remote_copy(
            src_ref=source,
            dst_ref=target,
            send_sem=send_sem.at[item, slot],
            recv_sem=recv_sem.at[item, slot],
            device_id=peer if axis is None else {axis: peer},
            device_id_type=pl.DeviceIdType.MESH,
        )

    copies = []
    relays = []
    for item, (axis, kind) in enumerate(plan):
        size = sizes[axis]
        if kind == "relay":
            half = size // 2
            core = lax.rem(me[axis], 2)
            place = me[axis] // 2
            sibling = me[axis] + 1 - 2 * core
            for step in range(1, half):
                peer = lax.rem(place + step, half) * 2 + core
                first = copy(item, step, ins[item], outs[item].at[me[axis]], axis, peer)
                first.start()
                origin = lax.rem(place + half - step, half) * 2 + core
                relays.append((item, step, first, axis, sibling, origin))
            own = copy(item, 0, ins[item], outs[item].at[me[axis]], axis, sibling)
            own.start()
            copies.append(own)
        elif kind == "spread":
            for rep_step in range(sizes["rep"]):
                for shard_step in range(sizes["shard"]):
                    if (rep_step, shard_step) != (0, 0):
                        peer = at(rep_step, shard_step)
                        target = outs[item].at[me["rep"], me["shard"]]
                        slot = rep_step * sizes["shard"] + shard_step
                        one = copy(item, slot, ins[item].at[peer["shard"]], target, None, peer)
                        one.start()
                        copies.append(one)
        else:
            for step in range(1, size):
                peer = lax.rem(me[axis] + step, size)
                source = ins[item] if kind == "gather" else ins[item].at[peer]
                one = copy(item, step, source, outs[item].at[me[axis]], axis, peer)
                one.start()
                copies.append(one)
    for item, (axis, kind) in enumerate(plan):
        if kind == "swap":
            outs[item][me[axis]] = ins[item][me[axis]]
        elif kind == "spread":
            outs[item][me["rep"], me["shard"]] = ins[item][me["shard"]]
        else:
            outs[item][me[axis]] = ins[item][...]
    for item, step, first, axis, sibling, origin in relays:
        first.wait_recv()
        block = outs[item].at[origin]
        second = copy(item, sizes[axis] // 2 + step, block, block, axis, sibling)
        second.start()
        copies.append(second)
    for one in copies:
        one.wait()
    for _, _, first, _, _, _ in relays:
        first.wait_send()


def exchange(sizes, number, *items):
    plan = tuple((axis, kind) for _, axis, kind in items)
    arrays = [array for array, _, _ in items]
    shapes = []
    for array, axis, kind in items:
        shape = array.shape if kind == "swap" else (sizes[axis],) + array.shape
        if kind == "spread":
            shape = (sizes["rep"],) + array.shape
        shapes.append(jax.ShapeDtypeStruct(shape, array.dtype))
    slots = max(sizes[axis] for axis, _ in plan)
    if any(kind == "spread" for _, kind in plan):
        slots = sizes["rep"] * sizes["shard"]
    vmem = pl.BlockSpec(memory_space=pltpu.VMEM)
    return pl.pallas_call(
        functools.partial(exchange_body, plan, sizes),
        out_shape=shapes,
        in_specs=[vmem] * len(arrays),
        out_specs=[vmem] * len(arrays),
        scratch_shapes=[
            pltpu.SemaphoreType.DMA((len(arrays), slots)),
            pltpu.SemaphoreType.DMA((len(arrays), slots)),
        ],
        compiler_params=pltpu.CompilerParams(collective_id=number, has_side_effects=True),
    )(*arrays)


def local(kernel, shapes, *arrays):
    vmem = pl.BlockSpec(memory_space=pltpu.VMEM)
    return pl.pallas_call(
        kernel,
        out_shape=shapes,
        in_specs=[vmem] * len(arrays),
        out_specs=[vmem] * len(shapes),
    )(*arrays)


def prepare_kernel(reps, shards, attn_in, fc_in, fc_out, w_in, w_ff):
    rank = lax.axis_index("rep")
    cols = w_in.shape[1] // 3
    piece = fc_out.shape[1] // reps
    width = cols * reps
    share = shards * piece
    for r in range(reps):

        @pl.when(rank == r)
        def _(r=r):
            for k in range(3):
                base = k * width + r * cols
                w_in[:, k * cols : (k + 1) * cols] = attn_in[0, :, base : base + cols]
            for k in range(shards):
                base = (k * reps + r) * piece
                w_ff[:, k * piece : (k + 1) * piece] = fc_in[0, :, base : base + piece]
            w_ff[:, share:] = fc_out[0, r * piece : (r + 1) * piece, :]


def finish_kernel(reps, shards, attn_all, out_all, ff_all, attn_in, attn_out, fc_in, fc_out):
    width = attn_out.shape[1]
    cols = width // reps
    piece = fc_out.shape[0] // reps
    share = shards * piece
    for r in range(reps):
        for k in range(3):
            base = k * width + r * cols
            attn_in[:, base : base + cols] = attn_all[r, :, k * cols : (k + 1) * cols].astype(F32)
        attn_out[:, r * cols : (r + 1) * cols] = out_all[r].astype(F32)
        for k in range(shards):
            base = (k * reps + r) * piece
            fc_in[:, base : base + piece] = ff_all[r, :, k * piece : (k + 1) * piece].astype(F32)
        fc_out[r * piece : (r + 1) * piece, :] = ff_all[r, :, share:].astype(F32)


def attend_kernel(heads, qkv, mixed, lse):
    cols = mixed.shape[1]
    depth = cols // heads
    scale = depth ** (-0.5)
    for h in range(heads):
        here = slice(h * depth, (h + 1) * depth)
        query = qkv[:, h * depth : (h + 1) * depth]
        key = qkv[:, cols + h * depth : cols + (h + 1) * depth]
        value = qkv[:, 2 * cols + h * depth : 2 * cols + (h + 1) * depth]
        scores = contract_cols(query, key) * scale
        top = jnp.max(scores, axis=-1, keepdims=True)
        total = top + jnp.log(jnp.sum(jnp.exp(scores - top), axis=-1, keepdims=True))
        probs = jnp.exp(scores - total).astype(BF16)
        mixed[:, here] = jnp.dot(probs, value, preferred_element_type=F32).astype(BF16)
        lse[:, h : h + 1] = total


def attend_back_kernel(heads, qkv, upstream, lse, grad, query_sum, value_sum):
    cols = upstream.shape[1]
    depth = cols // heads
    scale = depth ** (-0.5)
    for h in range(heads):
        first = slice(h * depth, (h + 1) * depth)
        second = slice(cols + h * depth, cols + (h + 1) * depth)
        third = slice(2 * cols + h * depth, 2 * cols + (h + 1) * depth)
        query, key, value, above = qkv[:, first], qkv[:, second], qkv[:, third], upstream[:, first]
        probs = jnp.exp(contract_cols(query, key) * scale - lse[:, h : h + 1])
        dprobs = contract_cols(above, value)
        delta = jnp.sum(probs * dprobs, axis=-1, keepdims=True)
        dscores = (probs * (dprobs - delta) * scale).astype(BF16)
        dquery = jnp.dot(dscores, key, preferred_element_type=F32)
        dvalue = contract_rows(probs.astype(BF16), above)
        grad[:, first] = dquery.astype(BF16)
        grad[:, second] = contract_rows(dscores, query).astype(BF16)
        grad[:, third] = dvalue.astype(BF16)
        query_sum[:, first] = jnp.sum(dquery, axis=0, keepdims=True)
        value_sum[:, first] = jnp.sum(dvalue, axis=0, keepdims=True)


def flat(blocks):
    return blocks.reshape((blocks.shape[0] * blocks.shape[1],) + blocks.shape[2:])


def split_body(
    sizes, hidden_in, attn_in, attn_out, fc_in, fc_out, norm_gains, biases, fc_in_bias, out_grad
):
    reps, shards = sizes["rep"], sizes["shard"]
    rank = lax.axis_index("rep")
    rows = hidden_in.shape[1]
    width = attn_out.shape[2]
    part = attn_out.shape[1]
    cols = width // reps
    units = fc_in.shape[2]
    share = units // reps
    piece = fc_out.shape[1] // reps
    heads = H // reps

    def mine(array, axis):
        return lax.dynamic_index_in_dim(array, rank, axis, keepdims=False)

    state = hidden_in[0].astype(F32)
    upstream = out_grad[0]
    w_in_part, w_ff_part = local(
        functools.partial(prepare_kernel, reps, shards),
        [
            jax.ShapeDtypeStruct((part, 3 * cols), BF16),
            jax.ShapeDtypeStruct((part, share + width), BF16),
        ],
        attn_in,
        fc_in,
        fc_out,
    )
    w_in, gains, shifts, up_bias, x_all, dy_low = exchange(
        sizes,
        0,
        (w_in_part, "shard", "relay"),
        (norm_gains[0], "shard", "gather"),
        (biases[0], "shard", "gather"),
        (fc_in_bias, "shard", "gather"),
        (hidden_in[0], "rep", "gather"),
        (upstream.astype(BF16), "rep", "gather"),
    )
    w_ff_part, w_in = lax.optimization_barrier((w_ff_part, w_in))
    w_ff = lax.all_gather(w_ff_part, "shard", axis=0, tiled=True)
    w_up, w_down = w_ff[:, :share], w_ff[:, share:]
    w_in, x_all, dy_low = flat(w_in), flat(x_all), flat(dy_low)
    gains = gains.astype(F32).swapaxes(0, 1).reshape(2, width)
    shifts = shifts.astype(F32).swapaxes(0, 1).reshape(6, width)
    up_bias = mine(up_bias.astype(F32).reshape(shards, reps, piece), 1).reshape(share)

    normed_all, normed1_all, inv1_all = norm_forward(x_all.astype(F32), gains[0], shifts[0])
    a_low = normed_all.astype(BF16)
    _, normed1, inv1 = norm_forward(state, gains[0], shifts[0])
    qkv = jnp.dot(a_low, w_in, preferred_element_type=F32)
    query_bias = mine(shifts[1].reshape(reps, cols), 0)
    value_bias = mine(shifts[2].reshape(reps, cols), 0)
    qkv = qkv + jnp.concatenate([query_bias, jnp.zeros_like(query_bias), value_bias])
    qkv = qkv.astype(BF16)
    attended, lse = local(
        functools.partial(attend_kernel, heads),
        [
            jax.ShapeDtypeStruct((reps * rows, cols), BF16),
            jax.ShapeDtypeStruct((reps * rows, heads), F32),
        ],
        qkv,
    )
    w_out, o_all = exchange(
        sizes, 1, (attn_out[0], "shard", "relay"), (attended, "rep", "gather")
    )
    w_out = flat(w_out)
    o_rows = lax.dynamic_slice_in_dim(o_all, rank * rows, rows, 1)
    o_rows = o_rows.swapaxes(0, 1).reshape(rows, width)
    mixed = state + jnp.dot(o_rows, w_out, preferred_element_type=F32) + shifts[3]
    normed_mid, normed2, inv2 = norm_forward(mixed, gains[1], shifts[4])
    (c_low,) = exchange(sizes, 2, (normed_mid.astype(BF16), "rep", "gather"))
    c_low = flat(c_low)
    pre = jnp.dot(c_low, w_up, preferred_element_type=F32) + up_bias
    act_low = jax.nn.gelu(pre, approximate=False).astype(BF16)
    y_part = jnp.dot(act_low, w_down, preferred_element_type=F32).astype(BF16)

    d_down = contract_rows(act_low, dy_low)
    dpre = contract_cols(dy_low, w_down) * gelu_slope(pre)
    dpre_low = dpre.astype(BF16)
    d_up_bias = jnp.sum(dpre, axis=0)
    dmid_part = contract_cols(dpre_low, w_up).astype(BF16)
    d_up = contract_rows(c_low, dpre_low)
    ff_grads = lax.psum_scatter(
        jnp.concatenate([d_up.astype(BF16), d_down.astype(BF16)], axis=1),
        "shard",
        scatter_dimension=0,
        tiled=True,
    )
    (dmid_parts,) = exchange(sizes, 3, (dmid_part.reshape(reps, rows, width), "rep", "swap"))
    dmid = jnp.sum(dmid_parts.astype(F32), axis=0)
    de5 = jnp.sum(upstream, axis=0)
    dmixed_part, dg2, de4 = norm_backward(dmid, gains[1], normed2, inv2)
    dmixed = upstream + dmixed_part
    de3 = jnp.sum(dmixed, axis=0)
    (dmixed_low,) = exchange(sizes, 4, (dmixed.astype(BF16), "rep", "gather"))
    dmixed_low = flat(dmixed_low)
    w_out_rows = mine(w_out.reshape(reps, cols, width), 0)
    dattended = contract_cols(dmixed_low, w_out_rows).astype(BF16)
    dmixed_cols = mine(dmixed_low.reshape(reps * rows, reps, cols), 1)
    d_out = jnp.einsum("rtc,td->rcd", o_all, dmixed_cols, preferred_element_type=F32)
    d_out = d_out.reshape(width, cols)

    g_qkv, de1, de2 = local(
        functools.partial(attend_back_kernel, heads),
        [
            jax.ShapeDtypeStruct((reps * rows, 3 * cols), BF16),
            jax.ShapeDtypeStruct((1, cols), F32),
            jax.ShapeDtypeStruct((1, cols), F32),
        ],
        qkv,
        dattended,
        lse,
    )
    de1, de2 = de1[0], de2[0]
    ff_grads, g_qkv = lax.optimization_barrier((ff_grads, g_qkv))
    ff_all = lax.all_gather(ff_grads, "rep", axis=0)
    dnormed_part = contract_cols(g_qkv, w_in).astype(BF16)
    d_qkv = contract_rows(a_low, g_qkv)
    d_out = lax.psum_scatter(d_out.astype(BF16), "shard", scatter_dimension=0, tiled=True)
    dnormed_parts, y_parts, attn_parts = exchange(
        sizes,
        5,
        (dnormed_part.reshape(reps, rows, width), "rep", "swap"),
        (y_part.reshape(reps, rows, width), "rep", "swap"),
        (d_qkv.astype(BF16).reshape(shards, part, 3 * cols), "shard", "swap"),
    )
    result = mixed + jnp.sum(y_parts.astype(F32), axis=0) + shifts[5]
    attn_sum = jnp.sum(attn_parts.astype(F32), axis=0).astype(BF16)
    dnormed = jnp.sum(dnormed_parts.astype(F32), axis=0)
    dstate_part, dg1, de0 = norm_backward(dnormed, gains[0], normed1, inv1)
    dstate = dmixed + dstate_part

    def placed(values):
        spread = jnp.zeros((reps, values.shape[0]), F32)
        return lax.dynamic_update_slice_in_dim(spread, values[None], rank, 0).reshape(-1)

    full = jnp.stack([dg1, dg2, de0, placed(de1), placed(de2), de3, de4, de5])
    full = full.reshape(8, shards, part).swapaxes(0, 1).reshape(shards, 8 * part)
    bias_parts = d_up_bias.reshape(shards, 1, piece)
    bias_parts = lax.dynamic_update_slice_in_dim(
        jnp.zeros((shards, reps, piece), F32), bias_parts, rank, 1
    ).reshape(shards, reps * piece)
    vectors = jnp.concatenate([full, bias_parts], axis=1)[:, None, :]
    attn_all, out_all, vectors = exchange(
        sizes,
        6,
        (attn_sum, "rep", "gather"),
        (d_out, "rep", "gather"),
        (vectors, "shard", "spread"),
    )
    vectors = jnp.sum(vectors, axis=(0, 1)).reshape(-1)
    g_attn_in, g_attn_out, g_fc_in, g_fc_out = local(
        functools.partial(finish_kernel, reps, shards),
        [
            jax.ShapeDtypeStruct((part, 3 * width), F32),
            jax.ShapeDtypeStruct((part, width), F32),
            jax.ShapeDtypeStruct((part, units), F32),
            jax.ShapeDtypeStruct((reps * piece, width), F32),
        ],
        attn_all,
        out_all,
        ff_all,
    )
    return (
        result[None],
        dstate[None],
        g_attn_in[None],
        g_attn_out[None],
        g_fc_in[None],
        g_fc_out[None],
        vectors[: 2 * part].reshape(1, 2, part),
        vectors[2 * part : 8 * part].reshape(1, 6, part),
        vectors[8 * part :][None],
    )


def run(sizes, *args):
    reps, shards = sizes["rep"], sizes["shard"]
    width, units = args[2].shape[2], args[3].shape[2]
    even = H % reps == 0 and shards % 2 == 0 and shards > 2 and reps > 1
    if args[1].shape[0] == 1 and args[0].shape[0] == 1 and even and units % (reps * shards) == 0:
        if width // reps * reps == width:
            return split_body(sizes, *args)
    return body(*args)


def solution(mesh):
    sizes = {axis: mesh.shape[axis] for axis in ("rep", "shard")}
    in_specs = (
        P("shard", "rep", None),
        P(None, "shard", None),
        P(None, "shard", None),
        P(None, "shard", None),
        P(None, "shard", None),
        P(None, None, "shard"),
        P(None, None, "shard"),
        P(None, "shard"),
        P("shard", "rep", None),
    )
    out_specs = (
        P("shard", "rep", None),
        P("shard", "rep", None),
        P(None, "shard", None),
        P(None, "shard", None),
        P(None, "shard", None),
        P(None, "shard", None),
        P(None, None, "shard"),
        P(None, None, "shard"),
        P(None, "shard"),
    )
    return jax.shard_map(
        functools.partial(run, sizes),
        mesh=mesh,
        in_specs=in_specs,
        out_specs=out_specs,
        check_vma=False,
    )
```

```python
import functools
import math

import jax
import jax.numpy as jnp
from jax import lax
from jax.experimental import pallas as pl
from jax.experimental.pallas import tpu as pltpu
from jax.sharding import PartitionSpec as P

H = 12

BF16 = jnp.bfloat16
F32 = jnp.float32


EPS = 1e-05


def norm_forward(values, gain, shift):
    center = values - jnp.mean(values, axis=-1, keepdims=True)
    inv_root = lax.rsqrt(jnp.mean(center * center, axis=-1, keepdims=True) + EPS)
    normed = center * inv_root
    return (normed * gain + shift, normed, inv_root)


def norm_backward(upstream, gain, normed, inv_root):
    scaled = upstream * gain
    inner = (
        scaled
        - jnp.mean(scaled, axis=-1, keepdims=True)
        - normed * jnp.mean(scaled * normed, axis=-1, keepdims=True)
    )
    return (inv_root * inner, jnp.sum(upstream * normed, axis=0), jnp.sum(upstream, axis=0))


def gelu_slope(pre):
    cdf = 0.5 * (1.0 + lax.erf(pre * (1.0 / math.sqrt(2.0))))
    dens = jnp.exp(-0.5 * pre * pre) * (1.0 / math.sqrt(2.0 * math.pi))
    return cdf + pre * dens


def contract_rows(left, right):
    return lax.dot_general(
        left, right, (((0,), (0,)), ((), ())), preferred_element_type=jnp.float32
    )


def contract_cols(left, right):
    return lax.dot_general(
        left, right, (((1,), (1,)), ((), ())), preferred_element_type=jnp.float32
    )


def split_heads(values):
    return values.reshape(values.shape[0], H, values.shape[1] // H)


def score_block(queries, keys):
    scale = (queries.shape[1] // H) ** (-0.5)
    return (
        jnp.einsum(
            "qhd,khd->hqk",
            split_heads(queries),
            split_heads(keys),
            preferred_element_type=jnp.float32,
        )
        * scale
    )


def attend(queries, keys, values_in):
    scores = score_block(queries, keys)
    top = jnp.max(scores, axis=-1, keepdims=True)
    lse = top[..., 0] + jnp.log(jnp.sum(jnp.exp(scores - top), axis=-1))
    probs = jnp.exp(scores - lse[..., None]).astype(jnp.bfloat16)
    mixed = jnp.einsum(
        "hqk,khd->qhd", probs, split_heads(values_in), preferred_element_type=jnp.float32
    )
    return (mixed.reshape(queries.shape[0], -1).astype(jnp.bfloat16), lse)


def attend_back(queries, keys, values_in, lse, upstream):
    scale = (queries.shape[1] // H) ** (-0.5)
    probs = jnp.exp(score_block(queries, keys) - lse[..., None])
    weights = probs.astype(jnp.bfloat16)
    dprobs = jnp.einsum(
        "qhd,khd->hqk",
        split_heads(upstream),
        split_heads(values_in),
        preferred_element_type=jnp.float32,
    )
    delta = jnp.sum(probs * dprobs, axis=-1, keepdims=True)
    dscores = (probs * (dprobs - delta) * scale).astype(jnp.bfloat16)
    dquery = jnp.einsum(
        "hqk,khd->qhd", dscores, split_heads(keys), preferred_element_type=jnp.float32
    ).reshape(queries.shape[0], -1)
    dkey = jnp.einsum(
        "hqk,qhd->khd", dscores, split_heads(queries), preferred_element_type=jnp.float32
    ).reshape(keys.shape[0], -1)
    dvalue = jnp.einsum(
        "hqk,qhd->khd", weights, split_heads(upstream), preferred_element_type=jnp.float32
    ).reshape(keys.shape[0], -1)
    return (dquery, dkey, dvalue)


def body(hidden_in, attn_in, attn_out, fc_in, fc_out, norm_gains, biases, fc_in_bias, out_grad):
    layers = attn_in.shape[0]
    state = hidden_in[0].astype(jnp.float32)
    layer = 0
    pieces = (
        lax.all_gather(attn_in[layer], "shard", axis=0, tiled=True),
        lax.all_gather(attn_out[layer], "shard", axis=0, tiled=True),
        lax.all_gather(fc_in[layer], "shard", axis=0, tiled=True),
        lax.all_gather(fc_out[layer], "shard", axis=0, tiled=True),
        lax.all_gather(norm_gains[layer], "shard", axis=1, tiled=True),
        lax.all_gather(biases[layer], "shard", axis=1, tiled=True),
        lax.all_gather(fc_in_bias[layer], "shard", axis=0, tiled=True),
    )
    w_qkv = pieces[0]
    w_out = pieces[1]
    w_up = pieces[2]
    w_down = pieces[3]
    gains = pieces[4].astype(jnp.float32)
    shifts = pieces[5].astype(jnp.float32)
    up_bias = pieces[6].astype(jnp.float32)
    width = w_out.shape[0]
    normed_in, normed1, inv1 = norm_forward(state, gains[0], shifts[0])
    a_low = normed_in.astype(jnp.bfloat16)
    qkv = jnp.dot(a_low, w_qkv, preferred_element_type=jnp.float32)
    queries = (qkv[:, :width] + shifts[1]).astype(jnp.bfloat16)
    keys_local = qkv[:, width : 2 * width].astype(jnp.bfloat16)
    values_local = (qkv[:, 2 * width :] + shifts[2]).astype(jnp.bfloat16)
    keys_all = lax.all_gather(keys_local, "rep", axis=0, tiled=True)
    values_all = lax.all_gather(values_local, "rep", axis=0, tiled=True)
    attended, lse = attend(queries, keys_all, values_all)
    mixed = state + jnp.dot(attended, w_out, preferred_element_type=jnp.float32) + shifts[3]
    normed_mid, normed2, inv2 = norm_forward(mixed, gains[1], shifts[4])
    c_low = normed_mid.astype(jnp.bfloat16)
    pre = jnp.dot(c_low, w_up, preferred_element_type=jnp.float32) + up_bias
    act_low = jax.nn.gelu(pre, approximate=False).astype(jnp.bfloat16)
    result = mixed + jnp.dot(act_low, w_down, preferred_element_type=jnp.float32) + shifts[5]
    saved = [
        (
            normed1,
            inv1,
            a_low,
            queries,
            keys_all,
            values_all,
            lse,
            attended,
            normed2,
            inv2,
            c_low,
            pre,
            act_low,
            (w_qkv, w_out, w_up, w_down, gains),
        )
    ]
    upstream = out_grad[0]
    layer_grads = [None] * layers
    for layer in reversed(range(layers)):
        (
            normed1,
            inv1,
            a_low,
            queries,
            keys_all,
            values_all,
            lse,
            attended,
            normed2,
            inv2,
            c_low,
            pre,
            act_low,
            held,
        ) = saved[layer]
        w_qkv, w_out, w_up, w_down, gains = held
        dy_low = upstream.astype(jnp.bfloat16)
        d_down = contract_rows(act_low, dy_low)
        de5 = jnp.sum(upstream, axis=0)
        dact = contract_cols(dy_low, w_down)
        dpre = dact * gelu_slope(pre)
        dpre_low = dpre.astype(jnp.bfloat16)
        d_up = contract_rows(c_low, dpre_low)
        d_up_bias = jnp.sum(dpre, axis=0)
        dmid = contract_cols(dpre_low, w_up)
        dmixed_part, dg2, de4 = norm_backward(dmid, gains[1], normed2, inv2)
        dmixed = upstream + dmixed_part
        dmixed_low = dmixed.astype(jnp.bfloat16)
        d_out = contract_rows(attended, dmixed_low)
        de3 = jnp.sum(dmixed, axis=0)
        dattended = contract_cols(dmixed_low, w_out).astype(jnp.bfloat16)
        dquery, dkey_part, dvalue_part = attend_back(queries, keys_all, values_all, lse, dattended)
        dkey, dvalue = (
            lax.psum_scatter(
                dkey_part.astype(jnp.bfloat16), "rep", scatter_dimension=0, tiled=True
            ).astype(jnp.float32),
            lax.psum_scatter(
                dvalue_part.astype(jnp.bfloat16), "rep", scatter_dimension=0, tiled=True
            ).astype(jnp.float32),
        )
        g_qkv = jnp.concatenate([dquery, dkey, dvalue], axis=1).astype(jnp.bfloat16)
        d_qkv = contract_rows(a_low, g_qkv)
        de1 = jnp.sum(dquery, axis=0)
        de2 = jnp.sum(dvalue, axis=0)
        dnormed = contract_cols(g_qkv, w_qkv)
        dstate_part, dg1, de0 = norm_backward(dnormed, gains[0], normed1, inv1)
        upstream = dmixed + dstate_part
        owned = (
            lax.psum_scatter(
                d_qkv.astype(jnp.bfloat16), "shard", scatter_dimension=0, tiled=True
            ).astype(jnp.float32),
            lax.psum_scatter(
                d_out.astype(jnp.bfloat16), "shard", scatter_dimension=0, tiled=True
            ).astype(jnp.float32),
            lax.psum_scatter(
                d_up.astype(jnp.bfloat16), "shard", scatter_dimension=0, tiled=True
            ).astype(jnp.float32),
            lax.psum_scatter(
                d_down.astype(jnp.bfloat16), "shard", scatter_dimension=0, tiled=True
            ).astype(jnp.float32),
            lax.psum_scatter(
                jnp.stack([dg1, dg2]).astype(jnp.bfloat16), "shard", scatter_dimension=1, tiled=True
            ).astype(jnp.float32),
            lax.psum_scatter(
                jnp.stack([de0, de1, de2, de3, de4, de5]).astype(jnp.bfloat16),
                "shard",
                scatter_dimension=1,
                tiled=True,
            ).astype(jnp.float32),
            lax.psum_scatter(
                d_up_bias.astype(jnp.bfloat16), "shard", scatter_dimension=0, tiled=True
            ).astype(jnp.float32),
        )
        owned = (
            lax.psum(owned[0].astype(jnp.bfloat16), "rep").astype(jnp.float32),
            lax.psum(owned[1].astype(jnp.bfloat16), "rep").astype(jnp.float32),
            lax.psum(owned[2].astype(jnp.bfloat16), "rep").astype(jnp.float32),
            lax.psum(owned[3].astype(jnp.bfloat16), "rep").astype(jnp.float32),
            lax.psum(owned[4].astype(jnp.bfloat16), "rep").astype(jnp.float32),
            lax.psum(owned[5].astype(jnp.bfloat16), "rep").astype(jnp.float32),
            lax.psum(owned[6].astype(jnp.bfloat16), "rep").astype(jnp.float32),
        )
        layer_grads[layer] = owned
    stacked = tuple((jnp.stack([grads[index] for grads in layer_grads]) for index in range(7)))
    return (
        result[None],
        upstream[None],
        stacked[0],
        stacked[1],
        stacked[2],
        stacked[3],
        stacked[4],
        stacked[5],
        stacked[6],
    )


def exchange_body(plan, sizes, *refs):
    count = len(plan)
    ins, outs = refs[:count], refs[count : 2 * count]
    send_sem, recv_sem = refs[2 * count :]
    me = {axis: lax.axis_index(axis) for axis in sizes}
    barrier = pltpu.get_barrier_semaphore()
    greeted = 0
    offsets = set()
    for axis, kind in plan:
        for rep_step in range(sizes["rep"]):
            for shard_step in range(sizes["shard"]):
                along = (shard_step if axis == "rep" else rep_step) == 0
                if (along or kind == "spread") and (rep_step, shard_step) != (0, 0):
                    offsets.add((rep_step, shard_step))

    def at(rep_step, shard_step):
        return {
            "rep": lax.rem(me["rep"] + rep_step, sizes["rep"]),
            "shard": lax.rem(me["shard"] + shard_step, sizes["shard"]),
        }

    for offset in sorted(offsets):
        pl.semaphore_signal(
            barrier, inc=1, device_id=at(*offset), device_id_type=pl.DeviceIdType.MESH
        )
        greeted += 1
    pl.semaphore_wait(barrier, greeted)

    def copy(item, slot, source, target, axis, peer):
        return pltpu.make_async_remote_copy(
            src_ref=source,
            dst_ref=target,
            send_sem=send_sem.at[item, slot],
            recv_sem=recv_sem.at[item, slot],
            device_id=peer if axis is None else {axis: peer},
            device_id_type=pl.DeviceIdType.MESH,
        )

    copies = []
    relays = []
    queues = [[] for _ in plan]
    for item, (axis, kind) in enumerate(plan):
        size = sizes[axis]
        if kind == "relay":
            half = size // 2
            core = lax.rem(me[axis], 2)
            place = me[axis] // 2
            sibling = me[axis] + 1 - 2 * core
            for step in range(1, half):
                peer = lax.rem(place + step, half) * 2 + core
                first = copy(item, step, ins[item], outs[item].at[me[axis]], axis, peer)
                queues[item].append(first)
                origin = lax.rem(place + half - step, half) * 2 + core
                relays.append((item, step, first, axis, sibling, origin))
            own = copy(item, 0, ins[item], outs[item].at[me[axis]], axis, sibling)
            queues[item].append(own)
            copies.append(own)
        elif kind == "spread":
            for rep_step in range(sizes["rep"]):
                for shard_step in range(sizes["shard"]):
                    if (rep_step, shard_step) != (0, 0):
                        peer = at(rep_step, shard_step)
                        target = outs[item].at[me["rep"], me["shard"]]
                        slot = rep_step * sizes["shard"] + shard_step
                        one = copy(item, slot, ins[item].at[peer["shard"]], target, None, peer)
                        queues[item].append(one)
                        copies.append(one)
        else:
            for step in range(1, size):
                peer = lax.rem(me[axis] + step, size)
                source = ins[item] if kind == "gather" else ins[item].at[peer]
                one = copy(item, step, source, outs[item].at[me[axis]], axis, peer)
                queues[item].append(one)
                copies.append(one)
    order = []
    for item, queue in enumerate(queues):
        order += [((2 * turn + 1) / len(queue), item, one) for turn, one in enumerate(queue)]
    for _, _, one in sorted(order, key=lambda entry: entry[:2]):
        one.start()
    for item, (axis, kind) in enumerate(plan):
        if kind == "swap":
            outs[item][me[axis]] = ins[item][me[axis]]
        elif kind == "spread":
            outs[item][me["rep"], me["shard"]] = ins[item][me["shard"]]
        else:
            outs[item][me[axis]] = ins[item][...]
    for item, step, first, axis, sibling, origin in relays:
        first.wait_recv()
        block = outs[item].at[origin]
        second = copy(item, sizes[axis] // 2 + step, block, block, axis, sibling)
        second.start()
        copies.append(second)
    for one in copies:
        one.wait()
    for _, _, first, _, _, _ in relays:
        first.wait_send()


def exchange(sizes, number, *items):
    plan = tuple((axis, kind) for _, axis, kind in items)
    arrays = [array for array, _, _ in items]
    shapes = []
    for array, axis, kind in items:
        shape = array.shape if kind == "swap" else (sizes[axis],) + array.shape
        if kind == "spread":
            shape = (sizes["rep"],) + array.shape
        shapes.append(jax.ShapeDtypeStruct(shape, array.dtype))
    slots = max(sizes[axis] for axis, _ in plan)
    if any(kind == "spread" for _, kind in plan):
        slots = sizes["rep"] * sizes["shard"]
    vmem = pl.BlockSpec(memory_space=pltpu.VMEM)
    return pl.pallas_call(
        functools.partial(exchange_body, plan, sizes),
        out_shape=shapes,
        in_specs=[vmem] * len(arrays),
        out_specs=[vmem] * len(arrays),
        scratch_shapes=[
            pltpu.SemaphoreType.DMA((len(arrays), slots)),
            pltpu.SemaphoreType.DMA((len(arrays), slots)),
        ],
        compiler_params=pltpu.CompilerParams(collective_id=number, has_side_effects=True),
    )(*arrays)


def local(kernel, shapes, *arrays):
    vmem = pl.BlockSpec(memory_space=pltpu.VMEM)
    return pl.pallas_call(
        kernel,
        out_shape=shapes,
        in_specs=[vmem] * len(arrays),
        out_specs=[vmem] * len(shapes),
    )(*arrays)


def prepare_kernel(reps, shards, attn_in, fc_in, fc_out, w_in, w_ff):
    rank = lax.axis_index("rep")
    cols = w_in.shape[1] // 3
    piece = fc_out.shape[0] // reps
    width = cols * reps
    share = shards * piece
    for r in range(reps):

        @pl.when(rank == r)
        def _(r=r):
            for k in range(3):
                base = k * width + r * cols
                w_in[:, k * cols : (k + 1) * cols] = attn_in[:, base : base + cols]
            for k in range(shards):
                base = (k * reps + r) * piece
                w_ff[:, k * piece : (k + 1) * piece] = fc_in[:, base : base + piece]
            w_ff[:, share:] = fc_out[r * piece : (r + 1) * piece, :]


def finish_kernel(reps, shards, attn_all, ff_all, attn_in, attn_out, fc_in, fc_out):
    width = attn_out.shape[1]
    cols = width // reps
    piece = fc_out.shape[0] // reps
    share = shards * piece
    for r in range(reps):
        for k in range(3):
            base = k * width + r * cols
            attn_in[:, base : base + cols] = attn_all[r, :, k * cols : (k + 1) * cols].astype(F32)
        attn_out[:, r * cols : (r + 1) * cols] = attn_all[r, :, 3 * cols :].astype(F32)
        for k in range(shards):
            base = (k * reps + r) * piece
            fc_in[:, base : base + piece] = ff_all[r, :, k * piece : (k + 1) * piece].astype(F32)
        fc_out[r * piece : (r + 1) * piece, :] = ff_all[r, :, share:].astype(F32)


def attend_kernel(heads, qkv, mixed, lse):
    cols = mixed.shape[1]
    depth = cols // heads
    scale = depth ** (-0.5)
    for h in range(heads):
        here = slice(h * depth, (h + 1) * depth)
        query = qkv[:, h * depth : (h + 1) * depth]
        key = qkv[:, cols + h * depth : cols + (h + 1) * depth]
        value = qkv[:, 2 * cols + h * depth : 2 * cols + (h + 1) * depth]
        scores = contract_cols(query, key) * scale
        top = jnp.max(scores, axis=-1, keepdims=True)
        total = top + jnp.log(jnp.sum(jnp.exp(scores - top), axis=-1, keepdims=True))
        probs = jnp.exp(scores - total).astype(BF16)
        mixed[:, here] = jnp.dot(probs, value, preferred_element_type=F32).astype(BF16)
        lse[:, h : h + 1] = total


def attend_back_kernel(heads, qkv, upstream, lse, grad, query_sum, value_sum):
    cols = upstream.shape[1]
    depth = cols // heads
    scale = depth ** (-0.5)
    for h in range(heads):
        first = slice(h * depth, (h + 1) * depth)
        second = slice(cols + h * depth, cols + (h + 1) * depth)
        third = slice(2 * cols + h * depth, 2 * cols + (h + 1) * depth)
        query, key, value, above = qkv[:, first], qkv[:, second], qkv[:, third], upstream[:, first]
        probs = jnp.exp(contract_cols(query, key) * scale - lse[:, h : h + 1])
        dprobs = contract_cols(above, value)
        delta = jnp.sum(probs * dprobs, axis=-1, keepdims=True)
        dscores = (probs * (dprobs - delta) * scale).astype(BF16)
        dquery = jnp.dot(dscores, key, preferred_element_type=F32)
        dvalue = contract_rows(probs.astype(BF16), above)
        grad[:, first] = dquery.astype(BF16)
        grad[:, second] = contract_rows(dscores, query).astype(BF16)
        grad[:, third] = dvalue.astype(BF16)
        query_sum[:, first] = jnp.sum(dquery, axis=0, keepdims=True)
        value_sum[:, first] = jnp.sum(dvalue, axis=0, keepdims=True)


def flat(blocks):
    return blocks.reshape((blocks.shape[0] * blocks.shape[1],) + blocks.shape[2:])


def split_body(
    sizes, hidden_in, attn_in, attn_out, fc_in, fc_out, norm_gains, biases, fc_in_bias, out_grad
):
    reps, shards = sizes["rep"], sizes["shard"]
    rank = lax.axis_index("rep")
    rows = hidden_in.shape[1]
    width = attn_out.shape[2]
    part = attn_out.shape[1]
    cols = width // reps
    units = fc_in.shape[2]
    share = units // reps
    piece = fc_out.shape[1] // reps
    heads = H // reps

    def mine(array, axis):
        return lax.dynamic_index_in_dim(array, rank, axis, keepdims=False)

    state = hidden_in[0].astype(F32)
    upstream = out_grad[0]
    w_in_part, w_ff_part = local(
        functools.partial(prepare_kernel, reps, shards),
        [
            jax.ShapeDtypeStruct((part, 3 * cols), BF16),
            jax.ShapeDtypeStruct((part, share + width), BF16),
        ],
        attn_in[0],
        fc_in[0],
        fc_out[0],
    )
    small = jnp.concatenate(
        [norm_gains[0].reshape(1, -1), biases[0].reshape(1, -1), fc_in_bias[0].reshape(1, -1)], axis=1
    )
    w_in, w_out, small, x_all, dy_low = exchange(
        sizes,
        0,
        (w_in_part, "shard", "relay"),
        (attn_out[0], "shard", "relay"),
        (small, "shard", "gather"),
        (hidden_in[0], "rep", "gather"),
        (upstream.astype(BF16), "rep", "gather"),
    )
    w_ff_part, w_in = lax.optimization_barrier((w_ff_part, w_in))
    w_ff = lax.all_gather(w_ff_part, "shard", axis=0, tiled=True)
    w_up, w_down = w_ff[:, :share], w_ff[:, share:]
    w_in, w_out, x_all, dy_low = flat(w_in), flat(w_out), flat(x_all), flat(dy_low)
    small = small[:, 0, :].astype(F32)
    gains = small[:, : 2 * part].reshape(shards, 2, part).swapaxes(0, 1).reshape(2, width)
    shifts = small[:, 2 * part : 8 * part].reshape(shards, 6, part).swapaxes(0, 1).reshape(6, width)
    up_bias = mine(small[:, 8 * part :].reshape(shards, reps, piece), 1).reshape(share)

    normed_all, normed1_all, inv1_all = norm_forward(x_all.astype(F32), gains[0], shifts[0])
    a_low = normed_all.astype(BF16)
    _, normed1, inv1 = norm_forward(state, gains[0], shifts[0])
    qkv = jnp.dot(a_low, w_in, preferred_element_type=F32)
    query_bias = mine(shifts[1].reshape(reps, cols), 0)
    value_bias = mine(shifts[2].reshape(reps, cols), 0)
    qkv = qkv + jnp.concatenate([query_bias, jnp.zeros_like(query_bias), value_bias])
    qkv = qkv.astype(BF16)
    attended, lse = local(
        functools.partial(attend_kernel, heads),
        [
            jax.ShapeDtypeStruct((reps * rows, cols), BF16),
            jax.ShapeDtypeStruct((reps * rows, heads), F32),
        ],
        qkv,
    )
    (o_all,) = exchange(sizes, 1, (attended, "rep", "gather"))
    o_rows = lax.dynamic_slice_in_dim(o_all, rank * rows, rows, 1)
    o_rows = o_rows.swapaxes(0, 1).reshape(rows, width)
    mixed = state + jnp.dot(o_rows, w_out, preferred_element_type=F32) + shifts[3]
    normed_mid, normed2, inv2 = norm_forward(mixed, gains[1], shifts[4])
    (c_low,) = exchange(sizes, 2, (normed_mid.astype(BF16), "rep", "gather"))
    c_low = flat(c_low)
    pre = jnp.dot(c_low, w_up, preferred_element_type=F32) + up_bias
    act_low = jax.nn.gelu(pre, approximate=False).astype(BF16)
    y_part = jnp.dot(act_low, w_down, preferred_element_type=F32).astype(BF16)

    d_down = contract_rows(act_low, dy_low)
    dpre = contract_cols(dy_low, w_down) * gelu_slope(pre)
    dpre_low = dpre.astype(BF16)
    d_up_bias = jnp.sum(dpre, axis=0)
    dmid_part = contract_cols(dpre_low, w_up).astype(BF16)
    d_up = contract_rows(c_low, dpre_low)
    ff_grads = lax.psum_scatter(
        jnp.concatenate([d_up.astype(BF16), d_down.astype(BF16)], axis=1),
        "shard",
        scatter_dimension=0,
        tiled=True,
    )
    (dmid_parts,) = exchange(sizes, 3, (dmid_part.reshape(reps, rows, width), "rep", "swap"))
    dmid = jnp.sum(dmid_parts.astype(F32), axis=0)
    de5 = jnp.sum(upstream, axis=0)
    dmixed_part, dg2, de4 = norm_backward(dmid, gains[1], normed2, inv2)
    dmixed = upstream + dmixed_part
    de3 = jnp.sum(dmixed, axis=0)
    (dmixed_low,) = exchange(sizes, 4, (dmixed.astype(BF16), "rep", "gather"))
    dmixed_low = flat(dmixed_low)
    w_out_rows = mine(w_out.reshape(reps, cols, width), 0)
    dattended = contract_cols(dmixed_low, w_out_rows).astype(BF16)
    dmixed_cols = mine(dmixed_low.reshape(reps * rows, reps, cols), 1)
    d_out = jnp.einsum("rtc,td->rcd", o_all, dmixed_cols, preferred_element_type=F32)
    d_out = d_out.reshape(width, cols)

    g_qkv, de1, de2 = local(
        functools.partial(attend_back_kernel, heads),
        [
            jax.ShapeDtypeStruct((reps * rows, 3 * cols), BF16),
            jax.ShapeDtypeStruct((1, cols), F32),
            jax.ShapeDtypeStruct((1, cols), F32),
        ],
        qkv,
        dattended,
        lse,
    )
    de1, de2 = de1[0], de2[0]
    dnormed_part = contract_cols(g_qkv, w_in).astype(BF16)
    d_qkv = contract_rows(a_low, g_qkv)
    attn_grads = jnp.concatenate([d_qkv.astype(BF16), d_out.astype(BF16)], axis=1)
    dnormed_parts, y_parts, ff_all, attn_parts = exchange(
        sizes,
        5,
        (dnormed_part.reshape(reps, rows, width), "rep", "swap"),
        (y_part.reshape(reps, rows, width), "rep", "swap"),
        (ff_grads, "rep", "gather"),
        (attn_grads.reshape(shards, part, width), "shard", "swap"),
    )
    result = mixed + jnp.sum(y_parts.astype(F32), axis=0) + shifts[5]
    attn_sum = jnp.sum(attn_parts.astype(F32), axis=0).astype(BF16)
    dnormed = jnp.sum(dnormed_parts.astype(F32), axis=0)
    dstate_part, dg1, de0 = norm_backward(dnormed, gains[0], normed1, inv1)
    dstate = dmixed + dstate_part

    def placed(values):
        spread = jnp.zeros((reps, values.shape[0]), F32)
        return lax.dynamic_update_slice_in_dim(spread, values[None], rank, 0).reshape(-1)

    full = jnp.stack([dg1, dg2, de0, placed(de1), placed(de2), de3, de4, de5])
    full = full.reshape(8, shards, part).swapaxes(0, 1).reshape(shards, 8 * part)
    bias_parts = d_up_bias.reshape(shards, 1, piece)
    bias_parts = lax.dynamic_update_slice_in_dim(
        jnp.zeros((shards, reps, piece), F32), bias_parts, rank, 1
    ).reshape(shards, reps * piece)
    vectors = jnp.concatenate([full, bias_parts], axis=1)[:, None, :]
    attn_all, vectors = exchange(
        sizes, 6, (attn_sum, "rep", "gather"), (vectors, "shard", "spread")
    )
    vectors = jnp.sum(vectors, axis=(0, 1)).reshape(-1)
    g_attn_in, g_attn_out, g_fc_in, g_fc_out = local(
        functools.partial(finish_kernel, reps, shards),
        [
            jax.ShapeDtypeStruct((part, 3 * width), F32),
            jax.ShapeDtypeStruct((part, width), F32),
            jax.ShapeDtypeStruct((part, units), F32),
            jax.ShapeDtypeStruct((reps * piece, width), F32),
        ],
        attn_all,
        ff_all,
    )
    return (
        result[None],
        dstate[None],
        g_attn_in[None],
        g_attn_out[None],
        g_fc_in[None],
        g_fc_out[None],
        vectors[: 2 * part].reshape(1, 2, part),
        vectors[2 * part : 8 * part].reshape(1, 6, part),
        vectors[8 * part :][None],
    )


def run(sizes, *args):
    reps, shards = sizes["rep"], sizes["shard"]
    width, units = args[2].shape[2], args[3].shape[2]
    even = H % reps == 0 and shards % 2 == 0 and shards > 2 and reps > 1
    if args[1].shape[0] == 1 and args[0].shape[0] == 1 and even and units % (reps * shards) == 0:
        if width // reps * reps == width:
            return split_body(sizes, *args)
    return body(*args)


def solution(mesh):
    sizes = {axis: mesh.shape[axis] for axis in ("rep", "shard")}
    in_specs = (
        P("shard", "rep", None),
        P(None, "shard", None),
        P(None, "shard", None),
        P(None, "shard", None),
        P(None, "shard", None),
        P(None, None, "shard"),
        P(None, None, "shard"),
        P(None, "shard"),
        P("shard", "rep", None),
    )
    out_specs = (
        P("shard", "rep", None),
        P("shard", "rep", None),
        P(None, "shard", None),
        P(None, "shard", None),
        P(None, "shard", None),
        P(None, "shard", None),
        P(None, None, "shard"),
        P(None, None, "shard"),
        P(None, "shard"),
    )
    return jax.shard_map(
        functools.partial(run, sizes),
        mesh=mesh,
        in_specs=in_specs,
        out_specs=out_specs,
        check_vma=False,
    )
```
